256 devices in a mesh: vel: 16 (over z, core), cx: 4 (over y), cy: 4 (over x).
Axes of the slice: x: 4, y: 4, z: 8, core: 2. Of those that a mesh axis runs over, the one named last changes fastest.
Arguments:
- distribution: float32 [64, 16, 4, 13824], P('cx', 'cy', None, 'vel'), may hold values from 0.1 to 2
- refine_level: int32 [64, 16, 4], P('cx', 'cy'), may hold values from 0 to 2, as said below
- gain_one: float32 [24, 24, 24], replicated, may hold values from 0 to 2
- gain_two: float32 [24, 24, 24], replicated, may hold values from 0 to 2
- loss_kernel: float32 [24, 24, 24], replicated, may hold values from 0 to 2
Outputs:
- evolved: float32 [64, 16, 4, 13824], P('cx', 'cy', None, 'vel')
The draws below stay inside these ranges and needn't reach their ends.
Inputs may be any that keep to these rules, and one draw needn't show every extreme that they name: `refine_level`: in each block of 256 cells (the 16 x 4 x 4 cells of one index of cx and cy) at most 128 cells have a level above 0, and some block has exactly 128.
All inputs are finite; a program needn't handle non-finite values.
Results may differ from the reference program's by a relative error of at most 0.0022.
Values may be sent and summed in bfloat16 or wider, within the bound.
A program may use at most 64 MiB of HBM per device.

```python
import math
import jax
import jax.numpy as jnp
from jax import lax

NV = 24
CX = 16
CY = 4
CZ = 4
VEL = 13824
NX = 64
NY = 16
NZ = 4
BLOCK = 256
BLOCKS = 16
ACT_MAX = 128


def draw_refine_level(key, part):
    key_count, key_full, key_rank, key_level = jax.random.split(key, 4)
    halving = jax.random.randint(key_count, (BLOCKS,), 0, 4)
    counts = jnp.right_shift(jnp.full((BLOCKS,), ACT_MAX, jnp.int32), halving)
    full_block = jax.random.randint(key_full, (), 0, BLOCKS)
    counts = jnp.where(jnp.arange(BLOCKS) == full_block, ACT_MAX, counts)
    rank_order = jax.vmap(lambda rank_key: jax.random.permutation(rank_key, BLOCK))(jax.random.split(key_rank, BLOCKS))
    active = rank_order < counts[:, None]
    levels = jax.random.randint(key_level, (BLOCKS, BLOCK), 1, 3) * active.astype(jnp.int32)
    level_grid = levels.reshape(NX // CX, NY // CY, CX, CY, CZ).transpose(0, 2, 1, 3, 4)
    return level_grid.reshape(NX, NY, NZ)


def block_scale(own_key, extent, pieces, smallest, largest):
    def one(axis_at, blocks):
        steps = jax.random.uniform(jax.random.fold_in(jax.random.fold_in(own_key, 6), axis_at), (blocks,), jnp.float32, smallest / len(pieces), largest / len(pieces))
        return jnp.repeat(jnp.exp(steps), extent[axis_at] // blocks).reshape((-1,) + (1,) * (len(extent) - axis_at - 1))

    level = one(*pieces[0])
    for cut in pieces[1:]:
        level = level * one(*cut)
    return level


def setup_inputs(seed: int = 0) -> dict:
    arg_keys = jax.random.split(jax.random.key(seed), 6)
    distribution = jnp.clip(jnp.exp(math.log(2.0) - 2.9957323 * jax.random.uniform(arg_keys[0], (NX, NY, NZ, VEL), jnp.float32) ** block_scale(arg_keys[0], (NX, NY, NZ, VEL), ((0, 4), (1, 4), (3, 16)), -0.2, 0.2)), 0.1, 2.0)
    refine_level = draw_refine_level(jax.random.fold_in(arg_keys[5], 71), 0)
    gain_one = jnp.clip(jax.random.uniform(arg_keys[2], (NV, NV, NV), jnp.float32, 0.0, 2.0), 0.0, 2.0)
    gain_two = jnp.clip(jax.random.uniform(arg_keys[3], (NV, NV, NV), jnp.float32, 0.0, 2.0), 0.0, 2.0)
    loss_kernel = jnp.clip(jax.random.uniform(arg_keys[4], (NV, NV, NV), jnp.float32, 0.0, 2.0), 0.0, 2.0)
    return {"distribution": distribution, "refine_level": refine_level, "gain_one": gain_one, "gain_two": gain_two, "loss_kernel": loss_kernel}


def dft_tables(points):
    indices = jnp.arange(points, dtype=jnp.int32)
    products = (indices[:, None] * indices[None, :]) % points
    angles = products.astype(jnp.float32) * (2.0 * math.pi / points)
    cosine = jnp.cos(angles)
    sine_table = jnp.sin(angles)
    forward = jnp.stack([jnp.stack([cosine, sine_table]), jnp.stack([-sine_table, cosine])])
    inverse = jnp.stack([jnp.stack([cosine, -sine_table]), jnp.stack([sine_table, cosine])])
    return forward.astype(jnp.bfloat16), inverse.astype(jnp.bfloat16)


def contract(pattern, left_side, right_side):
    return jnp.einsum(pattern, left_side.astype(jnp.float32), right_side.astype(jnp.float32))


def collide(cells, forward, inverse, gain_one, gain_two, loss_kernel):
    points = forward.shape[-1]
    cell_count = cells.shape[0]
    field = cells.reshape(cell_count, points, points, points)
    section_z = contract("nabz,qzw->qnabw", field, forward[:, 0]).astype(jnp.bfloat16)
    section_y = contract("pnayc,qpyw->qnawc", section_z, forward).astype(jnp.bfloat16)
    spectrum = contract("pnxbc,qpxw->qnwbc", section_y, forward)
    scale_factor = 1.0 / float(points ** 3)

    def filtered(kernel):
        weighted = (spectrum * (kernel * scale_factor)[None, None]).astype(jnp.bfloat16)
        back_x = contract("pnxbc,qpxw->qnwbc", weighted, inverse).astype(jnp.bfloat16)
        back_y = contract("pnayc,qpyw->qnawc", back_x, inverse).astype(jnp.bfloat16)
        return contract("pnabz,pzw->nabw", back_y, inverse[0])

    gain_term = filtered(gain_one) * filtered(gain_two)
    result = gain_term - field.astype(jnp.float32) * filtered(loss_kernel)
    return result.reshape(cell_count, points ** 3)


def courants(points, first_vel, local_count):
    vel_index = first_vel + jnp.arange(local_count, dtype=jnp.int32)
    index_x = vel_index // (points * points)
    index_y = (vel_index // points) % points
    index_z = vel_index % points

    def speed(index_part):
        return 0.3 * (2.0 * index_part.astype(jnp.float32) - (points - 1)) / (points - 1)

    return speed(index_x), speed(index_y), speed(index_z)


def upwind_flux(courant, center, lower_side, upper_side):
    return jnp.maximum(courant, 0.0) * (center - lower_side) + jnp.minimum(courant, 0.0) * (upper_side - center)


def reference(distribution, refine_level, gain_one, gain_two, loss_kernel):
    points = gain_one.shape[0]
    courant_x, courant_y, courant_z = courants(points, 0, points ** 3)
    fluxes = upwind_flux(courant_x, distribution, jnp.roll(distribution, 1, 0), jnp.roll(distribution, -1, 0))
    fluxes = fluxes + upwind_flux(courant_y, distribution, jnp.roll(distribution, 1, 1), jnp.roll(distribution, -1, 1))
    fluxes = fluxes + upwind_flux(courant_z, distribution, jnp.roll(distribution, 1, 2), jnp.roll(distribution, -1, 2))
    read = distribution - fluxes
    forward, inverse = dft_tables(points)
    cell_blocks = read.reshape(-1, BLOCK, points ** 3).astype(jnp.bfloat16)
    collision = lax.map(lambda cell_block: collide(cell_block, forward, inverse, gain_one, gain_two, loss_kernel), cell_blocks)
    collision = collision.reshape(read.shape)
    weight = 0.25 * refine_level.astype(jnp.float32)
    return read + weight[..., None] * collision
```

```python
import functools
import math

import jax
import jax.numpy as jnp
import numpy as np
from jax import lax
from jax.experimental import pallas as pl
from jax.experimental.pallas import tpu as pltpu
from jax.sharding import PartitionSpec as P

MESH = pl.DeviceIdType.MESH
F32, BF16 = jnp.float32, jnp.bfloat16
NV, NC = 24, 16
PLANE, HALF, LOCAL = NV * NV, NV * NV // 2, NV * NV * 3 // 2
FREQ = NV * NC
GROUPS, CELLS = 16, 8
ROWS = NV * CELLS
OUTER, MIDDLE = ((0, 384), (512, 352)), ((256, 384),)


def tables():
    jk = np.arange(PLANE)
    bc = np.arange(FREQ)
    turns = (np.outer(jk // NV, bc // NC) + np.outer(jk % NV, bc % NC)) % NV
    keep = (bc % NC <= NV // 2).astype(np.float64)
    twice = np.where((bc % NC == 0) | (bc % NC == NV // 2), 1.0, 2.0) * keep
    cosine = np.round(np.cos(2 * np.pi * turns / NV), 12)
    sine = np.round(np.sin(2 * np.pi * turns / NV), 12)
    forward = np.concatenate([cosine * keep, -sine * keep], 1)
    inverse = np.concatenate([(cosine * twice).T, (-sine * twice).T], 0)
    turns = np.outer(np.arange(NV), np.arange(NV)) % NV
    eye = np.eye(CELLS)
    along_x = np.concatenate(
        [
            np.kron(np.round(np.cos(2 * np.pi * turns / NV), 12), eye),
            np.kron(np.round(np.sin(2 * np.pi * turns / NV), 12), eye),
        ],
        0,
    )
    return tuple(jnp.asarray(t, dtype=BF16) for t in (forward, inverse, along_x))


def iota(shape, dim):
    return lax.broadcasted_iota(jnp.int32, shape, dim)


def dot(a, b):
    return jnp.dot(a, b, preferred_element_type=F32)


def kernel(
    dist, level, sym, forward_hbm, inverse_hbm, along_hbm, out,
    ext, read, send, recv, field, packed, result, forward, inverse, along,
    local_sem, table_sem, out_sem, face_send, face_recv, send_sem, recv_sem, back_send, back_recv,
):
    me = lax.axis_index("vel")
    my_x, my_y = lax.axis_index("cx"), lax.axis_index("cy")
    nx, ny = lax.axis_size("cx"), lax.axis_size("cy")
    x_low, x_high = {"cx": lax.rem(my_x + nx - 1, nx)}, {"cx": lax.rem(my_x + 1, nx)}
    y_low, y_high = {"cy": lax.rem(my_y + ny - 1, ny)}, {"cy": lax.rem(my_y + 1, ny)}
    falling = me < GROUPS // 2
    even = lax.rem(me, 2) == 0

    loads = [
        pltpu.make_async_copy(dist.at[0:8], ext.at[1:9, 1:5, 0:4], local_sem.at[0]),
        pltpu.make_async_copy(dist.at[8:16], ext.at[1:9, 1:5, 4:8], local_sem.at[1]),
        pltpu.make_async_copy(dist.at[8], ext.at[9, 1:5, 0:4], local_sem.at[2]),
        pltpu.make_async_copy(dist.at[7], ext.at[0, 1:5, 4:8], local_sem.at[3]),
    ]
    for load in loads:
        load.start()
    table_loads = [
        pltpu.make_async_copy(src, dst, table_sem.at[k])
        for k, (src, dst) in enumerate(
            ((forward_hbm, forward), (inverse_hbm, inverse), (along_hbm, along))
        )
    ]
    for load in table_loads:
        load.start()

    barrier = pltpu.get_barrier_semaphore()
    for there in (x_low, x_high, y_low, y_high):
        pl.semaphore_signal(barrier, inc=1, device_id=there, device_id_type=MESH)
    order = [8 + (k + 1) // 2 * (-1) ** k for k in range(GROUPS - 1)]
    for d in order:
        pl.semaphore_signal(
            barrier, inc=1, device_id={"vel": lax.rem(me + d, GROUPS)}, device_id_type=MESH
        )
    pl.semaphore_wait(barrier, GROUPS - 1 + 4)

    def remote(src, dst, send_at, recv_at, there):
        return pltpu.make_async_remote_copy(
            src_ref=src, dst_ref=dst, send_sem=send_at, recv_sem=recv_at,
            device_id=there, device_id_type=MESH,
        )

    def x_copy(up):
        if up:
            return remote(
                dist.at[0], ext.at[9, 1:5, 4:8], face_send.at[0], face_recv.at[0], x_low
            )
        return remote(dist.at[15], ext.at[0, 1:5, 0:4], face_send.at[0], face_recv.at[0], x_high)

    def y_copies(is_even):
        copies, at = [], 1
        for upper, segments in ((is_even, OUTER), (not is_even, MIDDLE)):
            for first, width in segments:
                for s in range(2):
                    lanes = pl.ds(first, width)
                    copies.append(
                        remote(
                            dist.at[8 * s : 8 * s + 8, 0 if upper else 3, :, lanes],
                            ext.at[1:9, 5 if upper else 0, 4 * s : 4 * s + 4, lanes],
                            face_send.at[at], face_recv.at[at], y_low if upper else y_high,
                        )
                    )
                    at += 1
        return copies

    for case in (True, False):

        @pl.when(even == case)
        def _():
            for copy in y_copies(case):
                copy.start()

    for case in (True, False):

        @pl.when(falling == case)
        def _():
            x_copy(case).start()

    levels = jnp.concatenate([level[y] for y in range(4)], axis=0).astype(F32).astype(BF16)
    r = iota((16, 256), 1)
    row = iota((16, 256), 0)
    x_hot = (row == lax.rem(r // 4, 2) * 8 + r // 32).astype(F32).astype(BF16)
    yz_hot = row == lax.rem(r // 8, 4) * 4 + lax.rem(r, 4)
    spread = dot(levels, x_hot)
    level_row = jnp.sum(jnp.where(yz_hot, spread, 0.0), axis=0, keepdims=True)
    active = (level_row > 0.5).astype(F32)
    upto = (iota((256, 256), 0) <= iota((256, 256), 1)).astype(F32).astype(BF16)
    slot = dot(jnp.broadcast_to(active, (8, 256)).astype(BF16), upto)[0:1] - 1.0
    hot = (
        (iota((128, 256), 0).astype(F32) == slot) & (jnp.broadcast_to(active, (128, 256)) > 0.5)
    ).astype(F32)
    picker = hot.astype(BF16)
    placer = (hot * (0.25 * level_row)).astype(BF16)

    lane = iota((1, LOCAL), 1) + me * LOCAL

    def speed(index):
        return 0.3 * (2.0 * index.astype(F32) - (NV - 1)) / (NV - 1)

    c_x = speed(lane // PLANE)
    c_y = speed(lax.rem(lane // NV, NV))
    c_z = speed(lax.rem(lane, NV))
    shape = (8, LOCAL)
    a_x, a_y, a_z = (jnp.broadcast_to(jnp.abs(c), shape) for c in (c_x, c_y, c_z))
    up_y, up_z = (jnp.broadcast_to(c, shape) > 0.0 for c in (c_y, c_z))
    z_at = lax.rem(iota(shape, 0), 4)
    first_z, last_z = z_at == 0, z_at == 3
    step_x = jnp.where(falling, 1, -1)

    for load in loads:
        load.wait()
    for case in (True, False):

        @pl.when(even == case)
        def _():
            for copy in y_copies(case):
                copy.wait()

    for case in (True, False):

        @pl.when(falling == case)
        def _():
            x_copy(case).wait()

    def plane(x, _):
        for y in range(4):
            f = ext[x + 1, y + 1]
            flux = a_x * (f - ext[x + 1 + step_x, y + 1])
            flux = flux + a_y * (f - jnp.where(up_y, ext[x + 1, y], ext[x + 1, y + 2]))
            low = jnp.where(first_z, pltpu.roll(f, 5, 0), pltpu.roll(f, 1, 0))
            high = jnp.where(last_z, pltpu.roll(f, 3, 0), pltpu.roll(f, 7, 0))
            flux = flux + a_z * (f - jnp.where(up_z, low, high))
            read[x, y] = f - flux
        return 0

    lax.fori_loop(0, 8, plane, 0)

    chosen = dot(picker, read[...].reshape(256, LOCAL).astype(BF16))
    send[...] = chosen.astype(BF16).reshape(GROUPS, CELLS, LOCAL)

    def exchange(there, send_sems, recv_sems):
        peer = lax.rem(me + there, GROUPS)
        return remote(
            send.at[peer], recv.at[me], send_sems.at[peer], recv_sems.at[me], {"vel": peer}
        )

    def arrived(d, recv_sems):
        peer = lax.rem(me + d, GROUPS)
        return remote(
            send.at[peer], recv.at[peer], send_sem.at[peer], recv_sems.at[peer], {"vel": peer}
        )

    for d in order:
        exchange(d, send_sem, recv_sem).start()
    recv[me] = send[me]
    for load in table_loads:
        load.wait()
    for d in order:
        arrived(d, recv_sem).wait_recv()

    for p in range(GROUPS // 2):
        left, right = recv[2 * p].astype(F32), recv[2 * p + 1].astype(F32)
        at = 3 * p * CELLS
        field[at : at + 8] = left[:, :PLANE]
        field[at + 8 : at + 16, :HALF] = left[:, PLANE:]
        field[at + 8 : at + 16, HALF:] = right[:, :HALF]
        field[at + 16 : at + 24] = right[:, HALF:]

    cells = field[...]
    section = dot(cells.astype(BF16), forward[...]).astype(BF16)
    turned = dot(along[...], section)
    spec_re = turned[:ROWS, :FREQ] + turned[ROWS:, FREQ:]
    spec_im = turned[:ROWS, FREQ:] - turned[ROWS:, :FREQ]
    filtered = []
    for k in range(3):
        weights = jnp.broadcast_to(
            sym[k * NV : (k + 1) * NV][:, None, :], (NV, CELLS, FREQ)
        ).reshape(ROWS, FREQ)
        weighted = jnp.concatenate([spec_re * weights, spec_im * weights], axis=1).astype(BF16)
        turned = dot(along[...], weighted)
        back = jnp.concatenate(
            [
                turned[:ROWS, :FREQ] - turned[ROWS:, FREQ:],
                turned[:ROWS, FREQ:] + turned[ROWS:, :FREQ],
            ],
            axis=1,
        ).astype(BF16)
        filtered.append(dot(back, inverse[...]))
    field[...] = filtered[0] * filtered[1] - cells * filtered[2]

    for d in order:
        peer = lax.rem(me + d, GROUPS)
        exchange(d, send_sem, recv_sem).wait_send()
    for p in range(GROUPS // 2):
        at = 3 * p * CELLS
        send[2 * p] = jnp.concatenate(
            [field[at : at + 8], field[at + 8 : at + 16, :HALF]], axis=1
        ).astype(BF16)
        send[2 * p + 1] = jnp.concatenate(
            [field[at + 8 : at + 16, HALF:], field[at + 16 : at + 24]], axis=1
        ).astype(BF16)

    def give_back(d):
        peer = lax.rem(me + d, GROUPS)
        return remote(
            send.at[peer], packed.at[me], back_send.at[peer], back_recv.at[me], {"vel": peer}
        )

    def came_back(d):
        peer = lax.rem(me + d, GROUPS)
        return remote(
            send.at[peer], packed.at[peer], back_send.at[peer], back_recv.at[peer], {"vel": peer}
        )

    for d in order:
        give_back(d).start()
    packed[me] = send[me]
    for d in order:
        came_back(d).wait_recv()

    rates = lax.dot_general(
        placer, packed[...].reshape(GROUPS * CELLS, LOCAL), (((0,), (0,)), ((), ())),
        preferred_element_type=F32,
    )
    result[...] = read[...] + rates.reshape(8, 4, 8, LOCAL)
    stores = [
        pltpu.make_async_copy(result.at[:, :, 0:4], out.at[0:8], out_sem.at[0]),
        pltpu.make_async_copy(result.at[:, :, 4:8], out.at[8:16], out_sem.at[1]),
    ]
    for store in stores:
        store.start()
    for d in order:
        give_back(d).wait_send()
    for store in stores:
        store.wait()


def frequency_weights(kernels):
    k = jnp.stack(kernels)
    other = jnp.roll(jnp.flip(k, (1, 2, 3)), 1, (1, 2, 3))
    k = (k + other)[..., : NV // 2 + 1] * (0.5 / float(NV**3))
    k = jnp.pad(k, ((0, 0), (0, 0), (0, 0), (0, NC - NV // 2 - 1)))
    return k.reshape(3 * NV, FREQ)


def per_device(distribution, refine_level, gain_one, gain_two, loss_kernel):
    sym = frequency_weights((gain_one, gain_two, loss_kernel))
    forward, inverse, along = tables()
    anywhere = pl.BlockSpec(memory_space=pl.ANY)
    vmem = pl.BlockSpec(memory_space=pltpu.VMEM)
    dma = pltpu.SemaphoreType.DMA
    return pl.pallas_call(
        kernel,
        out_shape=jax.ShapeDtypeStruct(distribution.shape, F32),
        in_specs=[anywhere, vmem, vmem, anywhere, anywhere, anywhere],
        out_specs=anywhere,
        scratch_shapes=[
            pltpu.VMEM((10, 6, 8, LOCAL), F32),
            pltpu.VMEM((8, 4, 8, LOCAL), F32),
            pltpu.VMEM((GROUPS, CELLS, LOCAL), BF16),
            pltpu.VMEM((GROUPS, CELLS, LOCAL), BF16),
            pltpu.VMEM((ROWS, PLANE), F32),
            pltpu.VMEM((GROUPS, CELLS, LOCAL), BF16),
            pltpu.VMEM((8, 4, 8, LOCAL), F32),
            pltpu.VMEM((PLANE, 2 * FREQ), BF16),
            pltpu.VMEM((2 * FREQ, PLANE), BF16),
            pltpu.VMEM((2 * ROWS, ROWS), BF16),
            dma((4,)), dma((3,)), dma((2,)), dma((7,)), dma((7,)),
            dma((GROUPS,)), dma((GROUPS,)), dma((GROUPS,)), dma((GROUPS,)),
        ],
        compiler_params=pltpu.CompilerParams(
            collective_id=0, has_side_effects=True, vmem_limit_bytes=48 << 20
        ),
    )(distribution, refine_level.transpose(1, 2, 0), sym, forward, inverse, along)


def solution(mesh):
    in_specs = (P("cx", "cy", None, "vel"), P("cx", "cy", None), P(), P(), P())
    return jax.shard_map(
        per_device, mesh=mesh, in_specs=in_specs,
        out_specs=P("cx", "cy", None, "vel"), check_vma=False,
    )
```

```python
import functools
import math

import jax
import jax.numpy as jnp
import numpy as np
from jax import lax
from jax.experimental import pallas as pl
from jax.experimental.pallas import tpu as pltpu
from jax.sharding import PartitionSpec as P

MESH = pl.DeviceIdType.MESH
F32, BF16 = jnp.float32, jnp.bfloat16
NV, NC = 24, 16
PLANE, HALF, LOCAL = NV * NV, NV * NV // 2, NV * NV * 3 // 2
FREQ = NV * NC
GROUPS, CELLS = 16, 8
ROWS = NV * CELLS
SEGMENTS = ((0, 384), (512, 352), (256, 384))
SEG = 384


def tables():
    jk = np.arange(PLANE)
    bc = np.arange(FREQ)
    turns = (np.outer(jk // NV, bc // NC) + np.outer(jk % NV, bc % NC)) % NV
    keep = (bc % NC <= NV // 2).astype(np.float64)
    twice = np.where((bc % NC == 0) | (bc % NC == NV // 2), 1.0, 2.0) * keep
    cosine = np.round(np.cos(2 * np.pi * turns / NV), 12)
    sine = np.round(np.sin(2 * np.pi * turns / NV), 12)
    forward = np.concatenate([cosine * keep, -sine * keep], 1)
    inverse = np.concatenate([(cosine * twice).T, (-sine * twice).T], 0)
    turns = np.outer(np.arange(NV), np.arange(NV)) % NV
    eye = np.eye(CELLS)
    along_x = np.concatenate(
        [
            np.kron(np.round(np.cos(2 * np.pi * turns / NV), 12), eye),
            np.kron(np.round(np.sin(2 * np.pi * turns / NV), 12), eye),
        ],
        0,
    )
    return tuple(jnp.asarray(t, dtype=BF16) for t in (forward, inverse, along_x))


def iota(shape, dim):
    return lax.broadcasted_iota(jnp.int32, shape, dim)


def dot(a, b):
    return jnp.dot(a, b, preferred_element_type=F32)


def kernel(
    dist, level_hbm, kernel_a, kernel_b, kernel_c, forward_hbm, inverse_hbm, along_hbm, out,
    ext, face, halo, read, send, recv, field, packed, forward, inverse, along, raw, spread, sym, level,
    local_sem, table_sem, hop_sem, face_send, face_recv, send_sem, recv_sem, back_send, back_recv,
):
    me = lax.axis_index("vel")
    my_x, my_y = lax.axis_index("cx"), lax.axis_index("cy")
    nx, ny = lax.axis_size("cx"), lax.axis_size("cy")
    x_low, x_high = {"cx": lax.rem(my_x + nx - 1, nx)}, {"cx": lax.rem(my_x + 1, nx)}
    y_low, y_high = {"cy": lax.rem(my_y + ny - 1, ny)}, {"cy": lax.rem(my_y + 1, ny)}
    falling = me < GROUPS // 2
    even = lax.rem(me, 2) == 0

    loads = [
        pltpu.make_async_copy(
            dist.at[8 * s : 8 * s + 8, y], ext.at[1:9, y + 1, 4 * s : 4 * s + 4], local_sem.at[2 * y + s]
        )
        for y in (0, 3, 1, 2)
        for s in range(2)
    ]
    loads += [
        pltpu.make_async_copy(dist.at[8], ext.at[9, 1:5, 0:4], local_sem.at[8]),
        pltpu.make_async_copy(dist.at[7], ext.at[0, 1:5, 4:8], local_sem.at[9]),
        pltpu.make_async_copy(level_hbm, level, local_sem.at[10]),
    ]
    for load in loads:
        load.start()
    table_loads = [
        pltpu.make_async_copy(src, dst, table_sem.at[k])
        for k, (src, dst) in enumerate(
            (
                (forward_hbm, forward), (inverse_hbm, inverse), (along_hbm, along),
                (kernel_a, raw.at[0:PLANE]), (kernel_b, raw.at[PLANE : 2 * PLANE]),
                (kernel_c, raw.at[2 * PLANE : 3 * PLANE]),
            )
        )
    ]

    barrier = pltpu.get_barrier_semaphore()
    twin = me + 1 - 2 * lax.rem(me, 2)
    near = [twin] + [lax.rem(m + d, GROUPS) for m in (me, twin) for d in (2, GROUPS - 2)]
    beside = [x_low, x_high, y_low, y_high] + [{"vel": v} for v in near]
    for there in beside:
        pl.semaphore_signal(barrier, inc=1, device_id=there, device_id_type=MESH)
    order = [8 + (k + 1) // 2 * (-1) ** k for k in range(GROUPS - 1)]

    def remote(src, dst, send_at, recv_at, there):
        return pltpu.make_async_remote_copy(
            src_ref=src, dst_ref=dst, send_sem=send_at, recv_sem=recv_at,
            device_id=there, device_id_type=MESH,
        )

    def x_copy(up):
        if up:
            return remote(
                dist.at[0], ext.at[9, 1:5, 4:8], face_send.at[0], face_recv.at[0], x_low
            )
        return remote(dist.at[15], ext.at[0, 1:5, 0:4], face_send.at[0], face_recv.at[0], x_high)

    def y_copies(is_even):
        outer = remote(
            face.at[0:2], halo.at[0:2], face_send.at[1], face_recv.at[1],
            y_low if is_even else y_high,
        )
        middle = remote(
            face.at[2], halo.at[2], face_send.at[2], face_recv.at[2],
            y_high if is_even else y_low,
        )
        return outer, middle

    for load in loads[:4]:
        load.wait()
    outer_y = jnp.where(even, 1, 4)
    for k, (first, width) in enumerate(SEGMENTS):
        y = 5 - outer_y if k == 2 else outer_y
        face[k, :, 0:width] = ext[1:9, y, :, first : first + width].reshape(64, width).astype(BF16)

    pl.semaphore_wait(barrier, len(beside))
    for case in (True, False):

        @pl.when(even == case)
        def _():
            for copy in y_copies(case):
                copy.start()

    for case in (True, False):

        @pl.when(falling == case)
        def _():
            x_copy(case).start()

    for load in table_loads:
        load.start()
    for k in range(3):
        for side, d in enumerate((2, GROUPS - 2)):
            pl.semaphore_signal(
                hop_sem.at[2 * k + side], inc=1, device_id={"vel": lax.rem(me + d, GROUPS)},
                device_id_type=MESH,
            )
        for side in range(2):
            pl.semaphore_wait(hop_sem.at[2 * k + side], 1)

    for load in loads[4:]:
        load.wait()
    levels = jnp.concatenate([level[y] for y in range(4)], axis=0).astype(F32).astype(BF16)
    r = iota((16, 256), 1)
    row = iota((16, 256), 0)
    x_hot = (row == lax.rem(r // 4, 2) * 8 + r // 32).astype(F32).astype(BF16)
    yz_hot = row == lax.rem(r // 8, 4) * 4 + lax.rem(r, 4)
    by_yz = dot(levels, x_hot)
    level_row = jnp.sum(jnp.where(yz_hot, by_yz, 0.0), axis=0, keepdims=True)
    active = (level_row > 0.5).astype(F32)
    upto = (iota((256, 256), 0) <= iota((256, 256), 1)).astype(F32).astype(BF16)
    slot = dot(jnp.broadcast_to(active, (8, 256)).astype(BF16), upto)[0:1] - 1.0
    hot = (
        (iota((128, 256), 0).astype(F32) == slot) & (jnp.broadcast_to(active, (128, 256)) > 0.5)
    ).astype(F32)
    picker = hot.astype(BF16)
    placer = (hot * (0.25 * level_row)).astype(BF16)

    lane = iota((1, LOCAL), 1) + me * LOCAL

    def speed(index):
        return 0.3 * (2.0 * index.astype(F32) - (NV - 1)) / (NV - 1)

    c_x = speed(lane // PLANE)
    c_y = speed(lax.rem(lane // NV, NV))
    c_z = speed(lax.rem(lane, NV))
    shape = (8, LOCAL)
    a_x, a_y, a_z = (jnp.broadcast_to(jnp.abs(c), shape) for c in (c_x, c_y, c_z))
    up_y, up_z = (jnp.broadcast_to(c, shape) > 0.0 for c in (c_y, c_z))
    z_at = lax.rem(iota(shape, 0), 4)
    first_z, last_z = z_at == 0, z_at == 3
    step_x = jnp.where(falling, 1, -1)

    for case in (True, False):

        @pl.when(even == case)
        def _():
            for copy in y_copies(case):
                copy.wait()

    outer_halo = jnp.where(even, 5, 0)
    for k, (first, width) in enumerate(SEGMENTS):
        y = 5 - outer_halo if k == 2 else outer_halo
        ext[1:9, y, :, first : first + width] = halo[k, :, 0:width].astype(F32).reshape(8, 8, width)

    for case in (True, False):

        @pl.when(falling == case)
        def _():
            x_copy(case).wait()

    def plane(x, _):
        for y in range(4):
            f = ext[x + 1, y + 1]
            flux = a_x * (f - ext[x + 1 + step_x, y + 1])
            flux = flux + a_y * (f - jnp.where(up_y, ext[x + 1, y], ext[x + 1, y + 2]))
            low = jnp.where(first_z, pltpu.roll(f, 5, 0), pltpu.roll(f, 1, 0))
            high = jnp.where(last_z, pltpu.roll(f, 3, 0), pltpu.roll(f, 7, 0))
            flux = flux + a_z * (f - jnp.where(up_z, low, high))
            read[x, y] = f - flux
        return 0

    lax.fori_loop(0, 8, plane, 0)

    chosen = dot(picker, read[...].reshape(256, LOCAL).astype(BF16))
    send[...] = chosen.astype(BF16).reshape(GROUPS, CELLS, LOCAL)

    def exchange(there, send_sems, recv_sems):
        peer = lax.rem(me + there, GROUPS)
        return remote(
            send.at[peer], recv.at[me], send_sems.at[peer], recv_sems.at[me], {"vel": peer}
        )

    def arrived(d, recv_sems):
        peer = lax.rem(me + d, GROUPS)
        return remote(
            send.at[peer], recv.at[peer], send_sem.at[peer], recv_sems.at[peer], {"vel": peer}
        )

    for d in order:
        exchange(d, send_sem, recv_sem).start()
    recv[me] = send[me]
    for load in table_loads:
        load.wait()

    for b in range(NV):
        spread[:, NV * b : NV * b + NV] = raw[pl.ds(b, 3 * NV, stride=NV), :]
    high = spread[...].astype(BF16)
    parts = jnp.concatenate([high, (spread[...] - high.astype(F32)).astype(BF16)], axis=0)
    at = iota((6 * NV, 6 * NV), 0)
    a_at = lax.rem(at, NV)
    turn = (iota((6 * NV, 6 * NV), 1) == at - a_at + lax.rem(NV - a_at, NV)).astype(F32).astype(BF16)
    turned = dot(turn, parts).astype(BF16)
    lane_b, lane_c = iota((1, FREQ), 1) // NC, lax.rem(iota((1, FREQ), 1), NC)
    used = lane_c <= NV // 2
    same = jnp.where(used, lane_b * NV + lane_c, -1)
    other = jnp.where(used, lax.rem(NV - lane_b, NV) * NV + lax.rem(NV - lane_c, NV), -1)
    pick = iota((PLANE, FREQ), 0)
    both = dot(parts, (pick == same).astype(F32).astype(BF16)) + dot(
        turned, (pick == other).astype(F32).astype(BF16)
    )
    sym[...] = (both[: 3 * NV] + both[3 * NV :]) * (0.5 / float(NV**3))

    for d in order:
        arrived(d, recv_sem).wait_recv()

    for p in range(GROUPS // 2):
        left, right = recv[2 * p].astype(F32), recv[2 * p + 1].astype(F32)
        at = 3 * p * CELLS
        field[at : at + 8] = left[:, :PLANE]
        field[at + 8 : at + 16, :HALF] = left[:, PLANE:]
        field[at + 8 : at + 16, HALF:] = right[:, :HALF]
        field[at + 16 : at + 24] = right[:, HALF:]

    cells = field[...]
    section = dot(cells.astype(BF16), forward[...]).astype(BF16)
    turned = dot(along[...], section)
    spec_re = turned[:ROWS, :FREQ] + turned[ROWS:, FREQ:]
    spec_im = turned[:ROWS, FREQ:] - turned[ROWS:, :FREQ]
    filtered = []
    for k in range(3):
        weights = jnp.broadcast_to(
            sym[k * NV : (k + 1) * NV][:, None, :], (NV, CELLS, FREQ)
        ).reshape(ROWS, FREQ)
        weighted = jnp.concatenate([spec_re * weights, spec_im * weights], axis=1).astype(BF16)
        turned = dot(along[...], weighted)
        back = jnp.concatenate(
            [
                turned[:ROWS, :FREQ] - turned[ROWS:, FREQ:],
                turned[:ROWS, FREQ:] + turned[ROWS:, :FREQ],
            ],
            axis=1,
        ).astype(BF16)
        filtered.append(dot(back, inverse[...]))
    field[...] = filtered[0] * filtered[1] - cells * filtered[2]

    for d in order:
        peer = lax.rem(me + d, GROUPS)
        exchange(d, send_sem, recv_sem).wait_send()
    for p in range(GROUPS // 2):
        at = 3 * p * CELLS
        send[2 * p] = jnp.concatenate(
            [field[at : at + 8], field[at + 8 : at + 16, :HALF]], axis=1
        ).astype(BF16)
        send[2 * p + 1] = jnp.concatenate(
            [field[at + 8 : at + 16, HALF:], field[at + 16 : at + 24]], axis=1
        ).astype(BF16)

    def give_back(d):
        peer = lax.rem(me + d, GROUPS)
        return remote(
            send.at[peer], packed.at[me], back_send.at[peer], back_recv.at[me], {"vel": peer}
        )

    def came_back(d):
        peer = lax.rem(me + d, GROUPS)
        return remote(
            send.at[peer], packed.at[peer], back_send.at[peer], back_recv.at[peer], {"vel": peer}
        )

    for d in order:
        give_back(d).start()
    packed[me] = send[me]
    for d in order:
        came_back(d).wait_recv()

    rates = lax.dot_general(
        placer, packed[...].reshape(GROUPS * CELLS, LOCAL), (((0,), (0,)), ((), ())),
        preferred_element_type=F32,
    )
    evolved = read[...] + rates.reshape(8, 4, 8, LOCAL)
    for part in range(2):
        out[8 * part : 8 * part + 8] = evolved[:, :, 4 * part : 4 * part + 4]
    for d in order:
        give_back(d).wait_send()


def in_hbm(array):
    return pltpu.with_memory_space_constraint(array, pltpu.MemorySpace.HBM)


def per_device(distribution, refine_level, gain_one, gain_two, loss_kernel):
    forward, inverse, along = tables()
    kernels = [k.reshape(PLANE, NV) for k in (gain_one, gain_two, loss_kernel)]
    hbm = pl.BlockSpec(memory_space=pltpu.MemorySpace.HBM)
    vmem = pl.BlockSpec(memory_space=pltpu.VMEM)
    dma = pltpu.SemaphoreType.DMA
    return pl.pallas_call(
        kernel,
        out_shape=pltpu.VMEM(distribution.shape, F32),
        in_specs=[hbm] * 8,
        out_specs=vmem,
        scratch_shapes=[
            pltpu.VMEM((10, 6, 8, LOCAL), F32),
            pltpu.VMEM((3, 64, SEG), BF16),
            pltpu.VMEM((3, 64, SEG), BF16),
            pltpu.VMEM((8, 4, 8, LOCAL), F32),
            pltpu.VMEM((GROUPS, CELLS, LOCAL), BF16),
            pltpu.VMEM((GROUPS, CELLS, LOCAL), BF16),
            pltpu.VMEM((ROWS, PLANE), F32),
            pltpu.VMEM((GROUPS, CELLS, LOCAL), BF16),
            pltpu.VMEM((PLANE, 2 * FREQ), BF16),
            pltpu.VMEM((2 * FREQ, PLANE), BF16),
            pltpu.VMEM((2 * ROWS, ROWS), BF16),
            pltpu.VMEM((3 * PLANE, NV), F32),
            pltpu.VMEM((3 * NV, PLANE), F32),
            pltpu.VMEM((3 * NV, FREQ), F32),
            pltpu.VMEM((4, 4, 16), jnp.int32),
            dma((11,)), dma((6,)), pltpu.SemaphoreType.REGULAR((6,)), dma((3,)), dma((3,)),
            dma((GROUPS,)), dma((GROUPS,)), dma((GROUPS,)), dma((GROUPS,)),
        ],
        compiler_params=pltpu.CompilerParams(
            collective_id=0, has_side_effects=True, vmem_limit_bytes=48 << 20
        ),
    )(*map(in_hbm, (distribution, refine_level.transpose(1, 2, 0), *kernels, forward, inverse, along)))


def solution(mesh):
    in_specs = (P("cx", "cy", None, "vel"), P("cx", "cy", None), P(), P(), P())
    return jax.shard_map(
        per_device, mesh=mesh, in_specs=in_specs,
        out_specs=P("cx", "cy", None, "vel"), check_vma=False,
    )
```

```python
import functools
import math

import jax
import jax.numpy as jnp
import numpy as np
from jax import lax
from jax.experimental import pallas as pl
from jax.experimental.pallas import tpu as pltpu
from jax.sharding import PartitionSpec as P

MESH = pl.DeviceIdType.MESH
F32, BF16 = jnp.float32, jnp.bfloat16
NV, NC = 24, 16
PLANE, HALF, LOCAL = NV * NV, NV * NV // 2, NV * NV * 3 // 2
FREQ = NV * NC
GROUPS, CHIPS, CELLS, TURNS = 16, 8, 4, 2
ROWS = NV * CELLS
SEGMENTS = ((0, 384), (512, 352), (256, 384))
SEG = 384


def tables():
    jk = np.arange(PLANE)
    bc = np.arange(FREQ)
    turns = (np.outer(jk // NV, bc // NC) + np.outer(jk % NV, bc % NC)) % NV
    keep = (bc % NC <= NV // 2).astype(np.float64)
    twice = np.where((bc % NC == 0) | (bc % NC == NV // 2), 1.0, 2.0) * keep
    cosine = np.round(np.cos(2 * np.pi * turns / NV), 12)
    sine = np.round(np.sin(2 * np.pi * turns / NV), 12)
    forward = np.concatenate([cosine * keep, -sine * keep], 1)
    inverse = np.concatenate([(cosine * twice).T, (-sine * twice).T], 0)
    row = np.arange(ROWS)
    i_at, i_cell = 3 * (row // CELLS % CHIPS) + row // (CELLS * CHIPS), row % CELLS
    a_at, a_cell = row % NV, row // NV
    turns = np.outer(a_at, i_at) % NV
    same = a_cell[:, None] == i_cell[None, :]
    cosine = np.round(np.cos(2 * np.pi * turns / NV), 12) * same
    sine = np.round(np.sin(2 * np.pi * turns / NV), 12) * same
    into_x = np.concatenate([cosine, sine], 0)
    from_x = np.concatenate([cosine.T, sine.T], 0)
    return tuple(jnp.asarray(t, dtype=BF16) for t in (forward, inverse, into_x, from_x))


def iota(shape, dim):
    return lax.broadcasted_iota(jnp.int32, shape, dim)


def dot(a, b):
    return jnp.dot(a, b, preferred_element_type=F32)


def kernel(
    dist, level_hbm, kernel_a, kernel_b, kernel_c, forward_hbm, inverse_hbm, into_hbm, from_hbm, out,
    ext, face, halo, read, send, recv, back, packed, forward, inverse, into_x, from_x, raw, spread, sym, level,
    local_sem, table_sem, hop_sem, face_send, face_recv, send_sem, recv_sem, back_send, back_recv,
):
    me = lax.axis_index("vel")
    my_x, my_y = lax.axis_index("cx"), lax.axis_index("cy")
    nx, ny = lax.axis_size("cx"), lax.axis_size("cy")
    x_low, x_high = {"cx": lax.rem(my_x + nx - 1, nx)}, {"cx": lax.rem(my_x + 1, nx)}
    y_low, y_high = {"cy": lax.rem(my_y + ny - 1, ny)}, {"cy": lax.rem(my_y + 1, ny)}
    falling = me < GROUPS // 2
    even = lax.rem(me, 2) == 0

    loads = [
        pltpu.make_async_copy(
            dist.at[8 * s : 8 * s + 8, y], ext.at[1:9, y + 1, 4 * s : 4 * s + 4], local_sem.at[2 * y + s]
        )
        for y in (0, 3, 1, 2)
        for s in range(2)
    ]
    loads += [
        pltpu.make_async_copy(dist.at[8], ext.at[9, 1:5, 0:4], local_sem.at[8]),
        pltpu.make_async_copy(dist.at[7], ext.at[0, 1:5, 4:8], local_sem.at[9]),
        pltpu.make_async_copy(level_hbm, level, local_sem.at[10]),
    ]
    for load in loads:
        load.start()
    table_loads = [
        pltpu.make_async_copy(src, dst, table_sem.at[k])
        for k, (src, dst) in enumerate(
            (
                (forward_hbm, forward), (inverse_hbm, inverse), (into_hbm, into_x), (from_hbm, from_x),
                (kernel_a, raw.at[0:PLANE]), (kernel_b, raw.at[PLANE : 2 * PLANE]),
                (kernel_c, raw.at[2 * PLANE : 3 * PLANE]),
            )
        )
    ]

    barrier = pltpu.get_barrier_semaphore()
    twin = me + 1 - 2 * lax.rem(me, 2)
    near = [twin] + [lax.rem(m + d, GROUPS) for m in (me, twin) for d in (2, GROUPS - 2)]
    beside = [x_low, x_high, y_low, y_high] + [{"vel": v} for v in near]
    for there in beside:
        pl.semaphore_signal(barrier, inc=1, device_id=there, device_id_type=MESH)
    order = [(dz, t) for dz in (4, 3, -3, 2, -2, 1, -1, 0) for t in (0, 1) if (dz, t) != (0, 0)]

    def partner(d):
        return lax.rem((twin if d[1] else me) + 2 * d[0] + GROUPS, GROUPS)


    def remote(src, dst, send_at, recv_at, there):
        return pltpu.make_async_remote_copy(
            src_ref=src, dst_ref=dst, send_sem=send_at, recv_sem=recv_at,
            device_id=there, device_id_type=MESH,
        )

    def x_copy(up):
        if up:
            return remote(
                dist.at[0], ext.at[9, 1:5, 4:8], face_send.at[0], face_recv.at[0], x_low
            )
        return remote(dist.at[15], ext.at[0, 1:5, 0:4], face_send.at[0], face_recv.at[0], x_high)

    def y_copies(is_even):
        outer = remote(
            face.at[0:2], halo.at[0:2], face_send.at[1], face_recv.at[1],
            y_low if is_even else y_high,
        )
        middle = remote(
            face.at[2], halo.at[2], face_send.at[2], face_recv.at[2],
            y_high if is_even else y_low,
        )
        return outer, middle

    for load in loads[:4]:
        load.wait()
    outer_y = jnp.where(even, 1, 4)
    for k, (first, width) in enumerate(SEGMENTS):
        y = 5 - outer_y if k == 2 else outer_y
        face[k, :, 0:width] = ext[1:9, y, :, first : first + width].reshape(64, width).astype(BF16)

    pl.semaphore_wait(barrier, len(beside))
    for case in (True, False):

        @pl.when(even == case)
        def _():
            for copy in y_copies(case):
                copy.start()

    for case in (True, False):

        @pl.when(falling == case)
        def _():
            x_copy(case).start()

    for load in table_loads:
        load.start()
    for k in range(3):
        for side, d in enumerate((2, GROUPS - 2)):
            pl.semaphore_signal(
                hop_sem.at[2 * k + side], inc=1, device_id={"vel": lax.rem(me + d, GROUPS)},
                device_id_type=MESH,
            )
        for side in range(2):
            pl.semaphore_wait(hop_sem.at[2 * k + side], 1)

    for load in loads[4:]:
        load.wait()
    levels = jnp.concatenate([level[y] for y in range(4)], axis=0).astype(F32).astype(BF16)
    r = iota((16, 256), 1)
    row = iota((16, 256), 0)
    x_hot = (row == lax.rem(r // 4, 2) * 8 + r // 32).astype(F32).astype(BF16)
    yz_hot = row == lax.rem(r // 8, 4) * 4 + lax.rem(r, 4)
    by_yz = dot(levels, x_hot)
    level_row = jnp.sum(jnp.where(yz_hot, by_yz, 0.0), axis=0, keepdims=True)
    active = (level_row > 0.5).astype(F32)
    upto = (iota((256, 256), 0) <= iota((256, 256), 1)).astype(F32).astype(BF16)
    slot = dot(jnp.broadcast_to(active, (8, 256)).astype(BF16), upto)[0:1] - 1.0
    hot = (
        (iota((128, 256), 0).astype(F32) == slot) & (jnp.broadcast_to(active, (128, 256)) > 0.5)
    ).astype(F32)
    picker = hot.astype(BF16)
    placer = (hot * (0.25 * level_row)).astype(BF16)

    lane = iota((1, LOCAL), 1) + me * LOCAL

    def speed(index):
        return 0.3 * (2.0 * index.astype(F32) - (NV - 1)) / (NV - 1)

    c_x = speed(lane // PLANE)
    c_y = speed(lax.rem(lane // NV, NV))
    c_z = speed(lax.rem(lane, NV))
    shape = (8, LOCAL)
    a_x, a_y, a_z = (jnp.broadcast_to(jnp.abs(c), shape) for c in (c_x, c_y, c_z))
    up_y, up_z = (jnp.broadcast_to(c, shape) > 0.0 for c in (c_y, c_z))
    z_at = lax.rem(iota(shape, 0), 4)
    first_z, last_z = z_at == 0, z_at == 3
    step_x = jnp.where(falling, 1, -1)

    for load in table_loads:
        load.wait()

    for b in range(NV):
        spread[:, NV * b : NV * b + NV] = raw[pl.ds(b, 3 * NV, stride=NV), :]
    high = spread[...].astype(BF16)
    parts = jnp.concatenate([high, (spread[...] - high.astype(F32)).astype(BF16)], axis=0)
    at = iota((6 * NV, 6 * NV), 0)
    a_at = lax.rem(at, NV)
    turn = (iota((6 * NV, 6 * NV), 1) == at - a_at + lax.rem(NV - a_at, NV)).astype(F32).astype(BF16)
    turned = dot(turn, parts).astype(BF16)
    lane_b, lane_c = iota((1, FREQ), 1) // NC, lax.rem(iota((1, FREQ), 1), NC)
    used = lane_c <= NV // 2
    same = jnp.where(used, lane_b * NV + lane_c, -1)
    other = jnp.where(used, lax.rem(NV - lane_b, NV) * NV + lax.rem(NV - lane_c, NV), -1)
    pick = iota((PLANE, FREQ), 0)
    both = dot(parts, (pick == same).astype(F32).astype(BF16)) + dot(
        turned, (pick == other).astype(F32).astype(BF16)
    )
    sym[...] = (both[: 3 * NV] + both[3 * NV :]) * (0.5 / float(NV**3))

    for case in (True, False):

        @pl.when(even == case)
        def _():
            for copy in y_copies(case):
                copy.wait()

    outer_halo = jnp.where(even, 5, 0)
    for k, (first, width) in enumerate(SEGMENTS):
        y = 5 - outer_halo if k == 2 else outer_halo
        ext[1:9, y, :, first : first + width] = halo[k, :, 0:width].astype(F32).reshape(8, 8, width)

    for case in (True, False):

        @pl.when(falling == case)
        def _():
            x_copy(case).wait()

    def plane(x, _):
        for y in range(4):
            f = ext[x + 1, y + 1]
            flux = a_x * (f - ext[x + 1 + step_x, y + 1])
            flux = flux + a_y * (f - jnp.where(up_y, ext[x + 1, y], ext[x + 1, y + 2]))
            low = jnp.where(first_z, pltpu.roll(f, 5, 0), pltpu.roll(f, 1, 0))
            high = jnp.where(last_z, pltpu.roll(f, 3, 0), pltpu.roll(f, 7, 0))
            flux = flux + a_z * (f - jnp.where(up_z, low, high))
            read[x, y] = f - flux
        return 0

    lax.fori_loop(0, 8, plane, 0)

    def block(ref, turn, device):
        return ref.at[turn, device // 2, pl.ds(pl.multiple_of(CELLS * lax.rem(device, 2), CELLS), CELLS)]

    def by_place(ref, turn, device):
        chip = device // 2
        rows = pl.ds(pl.multiple_of(CELLS * lax.rem(chip, 2), CELLS), CELLS)
        return ref.at[turn, lax.rem(device, 2), chip // 2, rows]

    def onward(turn, d):
        there = partner(d)
        return remote(
            block(send, turn, there), by_place(recv, turn, me),
            send_sem.at[turn, there], recv_sem.at[turn, me], {"vel": there},
        )

    def onward_from(turn, d):
        there = partner(d)
        return remote(
            block(send, turn, there), by_place(recv, turn, there),
            send_sem.at[turn, there], recv_sem.at[turn, there], {"vel": there},
        )

    def homeward(turn, d):
        there = partner(d)
        return remote(
            by_place(back, turn, there), block(packed, turn, me),
            back_send.at[turn, there], back_recv.at[turn, me], {"vel": there},
        )

    def homeward_from(turn, d):
        there = partner(d)
        return remote(
            by_place(back, turn, there), block(packed, turn, there),
            back_send.at[turn, there], back_recv.at[turn, there], {"vel": there},
        )

    values = read[...].reshape(256, LOCAL).astype(BF16)
    for turn in range(TURNS):
        chosen = dot(picker[64 * turn : 64 * turn + 64], values).astype(BF16)
        send[turn] = chosen.reshape(GROUPS // 2, 2 * CELLS, LOCAL)
        for d in order:
            onward(turn, d).start()
        own = pltpu.make_async_copy(
            block(send, turn, me), by_place(recv, turn, me), send_sem.at[turn, me]
        )
        own.start()

    for turn in range(TURNS):
        pltpu.make_async_copy(
            block(send, turn, me), by_place(recv, turn, me), send_sem.at[turn, me]
        ).wait()
        for d in order:
            onward_from(turn, d).wait_recv()
        left, right = (recv[turn, core].reshape(CHIPS * CELLS, LOCAL).astype(F32) for core in range(2))
        cells = jnp.concatenate(
            [
                left[:, :PLANE],
                jnp.concatenate([left[:, PLANE:], right[:, :HALF]], axis=1),
                right[:, HALF:],
            ],
            axis=0,
        )
        section = dot(cells.astype(BF16), forward[...]).astype(BF16)
        turned = dot(into_x[...], section)
        spec_re = turned[:ROWS, :FREQ] + turned[ROWS:, FREQ:]
        spec_im = turned[:ROWS, FREQ:] - turned[ROWS:, :FREQ]
        spectra = []
        for k in range(3):
            weights = sym[k * NV : (k + 1) * NV]
            weights = jnp.concatenate([weights] * CELLS, axis=0)
            weighted = jnp.concatenate([spec_re * weights, spec_im * weights], axis=1).astype(BF16)
            turned = dot(from_x[...], weighted)
            spectra.append(
                jnp.concatenate(
                    [
                        turned[:ROWS, :FREQ] - turned[ROWS:, FREQ:],
                        turned[:ROWS, FREQ:] + turned[ROWS:, :FREQ],
                    ],
                    axis=1,
                ).astype(BF16)
            )
        filtered = dot(jnp.concatenate(spectra, axis=0), inverse[...])
        terms = filtered[:ROWS] * filtered[ROWS : 2 * ROWS] - cells * filtered[2 * ROWS :]
        third = CHIPS * CELLS
        low, middle, high = (terms[third * q : third * q + third] for q in range(3))
        back[turn, 0] = jnp.concatenate([low, middle[:, :HALF]], axis=1).astype(BF16).reshape(
            CHIPS // 2, 2 * CELLS, LOCAL
        )
        back[turn, 1] = jnp.concatenate([middle[:, HALF:], high], axis=1).astype(BF16).reshape(
            CHIPS // 2, 2 * CELLS, LOCAL
        )
        for d in order:
            homeward(turn, d).start()
        pltpu.make_async_copy(
            by_place(back, turn, me), block(packed, turn, me), back_send.at[turn, me]
        ).start()

    for turn in range(TURNS):
        pltpu.make_async_copy(
            by_place(back, turn, me), block(packed, turn, me), back_send.at[turn, me]
        ).wait()
        for d in order:
            homeward_from(turn, d).wait_recv()

    rates = lax.dot_general(
        placer, packed[...].reshape(TURNS * GROUPS * CELLS, LOCAL), (((0,), (0,)), ((), ())),
        preferred_element_type=F32,
    )
    evolved = read[...] + rates.reshape(8, 4, 8, LOCAL)
    for part in range(2):
        out[8 * part : 8 * part + 8] = evolved[:, :, 4 * part : 4 * part + 4]
    for turn in range(TURNS):
        for d in order:
            onward(turn, d).wait_send()
            homeward(turn, d).wait_send()


def in_hbm(array):
    return pltpu.with_memory_space_constraint(array, pltpu.MemorySpace.HBM)


def per_device(distribution, refine_level, gain_one, gain_two, loss_kernel):
    constants = tables()
    kernels = [k.reshape(PLANE, NV) for k in (gain_one, gain_two, loss_kernel)]
    hbm = pl.BlockSpec(memory_space=pltpu.MemorySpace.HBM)
    vmem = pl.BlockSpec(memory_space=pltpu.VMEM)
    dma = pltpu.SemaphoreType.DMA
    return pl.pallas_call(
        kernel,
        out_shape=pltpu.VMEM(distribution.shape, F32),
        in_specs=[hbm] * 9,
        out_specs=vmem,
        scratch_shapes=[
            pltpu.VMEM((10, 6, 8, LOCAL), F32),
            pltpu.VMEM((3, 64, SEG), BF16),
            pltpu.VMEM((3, 64, SEG), BF16),
            pltpu.VMEM((8, 4, 8, LOCAL), F32),
            pltpu.VMEM((TURNS, GROUPS // 2, 2 * CELLS, LOCAL), BF16),
            pltpu.VMEM((TURNS, 2, CHIPS // 2, 2 * CELLS, LOCAL), BF16),
            pltpu.VMEM((TURNS, 2, CHIPS // 2, 2 * CELLS, LOCAL), BF16),
            pltpu.VMEM((TURNS, GROUPS // 2, 2 * CELLS, LOCAL), BF16),
            pltpu.VMEM((PLANE, 2 * FREQ), BF16),
            pltpu.VMEM((2 * FREQ, PLANE), BF16),
            pltpu.VMEM((2 * ROWS, ROWS), BF16),
            pltpu.VMEM((2 * ROWS, ROWS), BF16),
            pltpu.VMEM((3 * PLANE, NV), F32),
            pltpu.VMEM((3 * NV, PLANE), F32),
            pltpu.VMEM((3 * NV, FREQ), F32),
            pltpu.VMEM((4, 4, 16), jnp.int32),
            dma((11,)), dma((7,)), pltpu.SemaphoreType.REGULAR((6,)), dma((3,)), dma((3,)),
            *[dma((TURNS, GROUPS))] * 4,
        ],
        compiler_params=pltpu.CompilerParams(
            collective_id=0, has_side_effects=True, vmem_limit_bytes=48 << 20
        ),
    )(*map(in_hbm, (distribution, refine_level.transpose(1, 2, 0), *kernels, *constants)))


def solution(mesh):
    in_specs = (P("cx", "cy", None, "vel"), P("cx", "cy", None), P(), P(), P())
    return jax.shard_map(
        per_device, mesh=mesh, in_specs=in_specs,
        out_specs=P("cx", "cy", None, "vel"), check_vma=False,
    )
```

```python
import functools
import math

import jax
import jax.numpy as jnp
import numpy as np
from jax import lax
from jax.experimental import pallas as pl
from jax.experimental.pallas import tpu as pltpu
from jax.sharding import PartitionSpec as P

MESH = pl.DeviceIdType.MESH
F32, BF16 = jnp.float32, jnp.bfloat16
NV, NC = 24, 16
PLANE, HALF, LOCAL = NV * NV, NV * NV // 2, NV * NV * 3 // 2
FREQ = NV * NC
GROUPS, CHIPS, CELLS, TURNS = 16, 8, 4, 2
ROWS = NV * CELLS
SEGMENTS = ((0, 384), (512, 352), (256, 384))
SEG = 384
Y_ORDER = (1, 2, 0, 3)


def tables():
    jk = np.arange(PLANE)
    bc = np.arange(FREQ)
    turns = (np.outer(jk // NV, bc // NC) + np.outer(jk % NV, bc % NC)) % NV
    keep = (bc % NC <= NV // 2).astype(np.float64)
    twice = np.where((bc % NC == 0) | (bc % NC == NV // 2), 1.0, 2.0) * keep
    cosine = np.round(np.cos(2 * np.pi * turns / NV), 12)
    sine = np.round(np.sin(2 * np.pi * turns / NV), 12)
    forward = np.concatenate([cosine * keep, -sine * keep], 1)
    inverse = np.concatenate([(cosine * twice).T, (-sine * twice).T], 0)
    row = np.arange(ROWS)
    i_at, i_cell = 3 * (row // CELLS % CHIPS) + row // (CELLS * CHIPS), row % CELLS
    a_at, a_cell = row % NV, row // NV
    turns = np.outer(a_at, i_at) % NV
    same = a_cell[:, None] == i_cell[None, :]
    cosine = np.round(np.cos(2 * np.pi * turns / NV), 12) * same
    sine = np.round(np.sin(2 * np.pi * turns / NV), 12) * same
    into_x = np.concatenate([cosine, sine], 0)
    from_x = np.concatenate([cosine.T, sine.T], 0)
    return tuple(jnp.asarray(t, dtype=BF16) for t in (forward, inverse, into_x, from_x))


def iota(shape, dim):
    return lax.broadcasted_iota(jnp.int32, shape, dim)


def dot(a, b):
    return jnp.dot(a, b, preferred_element_type=F32)


def kernel(
    dist, level_hbm, kernel_a, kernel_b, kernel_c, forward_hbm, inverse_hbm, into_hbm, from_hbm, out,
    ext, face, halo, edge_out, edge_in, read, values, send, recv, back, packed, forward, inverse, into_x, from_x, raw, spread, sym, level,
    local_sem, table_sem, hop_sem, face_send, face_recv, send_sem, recv_sem, back_send, back_recv,
):
    me = lax.axis_index("vel")
    my_x, my_y = lax.axis_index("cx"), lax.axis_index("cy")
    nx, ny = lax.axis_size("cx"), lax.axis_size("cy")
    x_low, x_high = {"cx": lax.rem(my_x + nx - 1, nx)}, {"cx": lax.rem(my_x + 1, nx)}
    y_low, y_high = {"cy": lax.rem(my_y + ny - 1, ny)}, {"cy": lax.rem(my_y + 1, ny)}
    falling = me < GROUPS // 2
    even = lax.rem(me, 2) == 0

    loads = [
        pltpu.make_async_copy(
            dist.at[8 * s : 8 * s + 8, y], ext.at[1:9, y + 1, 4 * s : 4 * s + 4], local_sem.at[2 * y + s]
        )
        for y in (0, 3, 1, 2)
        for s in range(2)
    ]
    loads += [
        pltpu.make_async_copy(dist.at[8], ext.at[9, 1:5, 0:4], local_sem.at[8]),
        pltpu.make_async_copy(dist.at[7], ext.at[0, 1:5, 4:8], local_sem.at[9]),
        pltpu.make_async_copy(level_hbm, level, local_sem.at[10]),
    ]
    for load in loads:
        load.start()
    table_loads = [
        pltpu.make_async_copy(src, dst, table_sem.at[k])
        for k, (src, dst) in enumerate(
            (
                (forward_hbm, forward), (inverse_hbm, inverse), (into_hbm, into_x), (from_hbm, from_x),
                (kernel_a, raw.at[0:PLANE]), (kernel_b, raw.at[PLANE : 2 * PLANE]),
                (kernel_c, raw.at[2 * PLANE : 3 * PLANE]),
            )
        )
    ]

    barrier = pltpu.get_barrier_semaphore()
    twin = me + 1 - 2 * lax.rem(me, 2)
    near = [twin] + [lax.rem(m + d, GROUPS) for m in (me, twin) for d in (2, GROUPS - 2)]
    beside = [x_low, x_high, y_low, y_high] + [{"vel": v} for v in near]
    for there in beside:
        pl.semaphore_signal(barrier, inc=1, device_id=there, device_id_type=MESH)
    order = [(dz, t) for dz in (4, 3, -3, 2, -2, 1, -1, 0) for t in (0, 1) if (dz, t) != (0, 0)]

    def partner(d):
        return lax.rem((twin if d[1] else me) + 2 * d[0] + GROUPS, GROUPS)


    def remote(src, dst, send_at, recv_at, there):
        return pltpu.make_async_remote_copy(
            src_ref=src, dst_ref=dst, send_sem=send_at, recv_sem=recv_at,
            device_id=there, device_id_type=MESH,
        )

    def x_copy(up):
        return remote(edge_out, edge_in, face_send.at[0], face_recv.at[0], x_low if up else x_high)

    def y_copies(is_even):
        outer = remote(
            face.at[0:2], halo.at[0:2], face_send.at[1], face_recv.at[1],
            y_low if is_even else y_high,
        )
        middle = remote(
            face.at[2], halo.at[2], face_send.at[2], face_recv.at[2],
            y_high if is_even else y_low,
        )
        return outer, middle

    for load in loads[:4]:
        load.wait()
    outer_y = jnp.where(even, 1, 4)
    for k, (first, width) in enumerate(SEGMENTS):
        y = 5 - outer_y if k == 2 else outer_y
        face[k, :, 0:width] = ext[1:9, y, :, first : first + width].reshape(64, width).astype(BF16)

    for load in loads[4:]:
        load.wait()
    edge = jnp.where(falling, ext[1, 1:5, 0:4], ext[8, 1:5, 4:8])
    edge_out[...] = edge.reshape(16, LOCAL).astype(BF16)

    pl.semaphore_wait(barrier, len(beside))
    for case in (True, False):

        @pl.when(even == case)
        def _():
            for copy in y_copies(case):
                copy.start()

    for case in (True, False):

        @pl.when(falling == case)
        def _():
            x_copy(case).start()

    for load in table_loads:
        load.start()
    def tell(k):
        for side, d in enumerate((2, GROUPS - 2)):
            pl.semaphore_signal(
                hop_sem.at[2 * k + side], inc=1, device_id={"vel": lax.rem(me + d, GROUPS)},
                device_id_type=MESH,
            )

    def hear(k):
        for side in range(2):
            pl.semaphore_wait(hop_sem.at[2 * k + side], 1)

    tell(0)

    levels = jnp.concatenate([level[y] for y in range(4)], axis=0).astype(F32).astype(BF16)
    r = iota((16, 256), 1)
    row = iota((16, 256), 0)
    x_hot = (row == lax.rem(r // 4, 2) * 8 + r // 32).astype(F32).astype(BF16)
    y_rank = lax.rem(r // 8, 4)
    yz_hot = row == jnp.where(y_rank < 2, y_rank + 1, 3 * y_rank - 6) * 4 + lax.rem(r, 4)
    by_yz = dot(levels, x_hot)
    level_row = jnp.sum(jnp.where(yz_hot, by_yz, 0.0), axis=0, keepdims=True)
    active = (level_row > 0.5).astype(F32)
    upto = (iota((256, 256), 0) <= iota((256, 256), 1)).astype(F32).astype(BF16)
    slot = dot(jnp.broadcast_to(active, (8, 256)).astype(BF16), upto)[0:1] - 1.0
    hot = (
        (iota((128, 256), 0).astype(F32) == slot) & (jnp.broadcast_to(active, (128, 256)) > 0.5)
    ).astype(F32)
    picker = hot.astype(BF16)
    placer = (hot * (0.25 * level_row)).astype(BF16)

    lane = iota((1, LOCAL), 1) + me * LOCAL

    def speed(index):
        return 0.3 * (2.0 * index.astype(F32) - (NV - 1)) / (NV - 1)

    c_x = speed(lane // PLANE)
    c_y = speed(lax.rem(lane // NV, NV))
    c_z = speed(lax.rem(lane, NV))
    shape = (8, LOCAL)
    a_x, a_y, a_z = (jnp.broadcast_to(jnp.abs(c), shape) for c in (c_x, c_y, c_z))
    up_y, up_z = (jnp.broadcast_to(c, shape) > 0.0 for c in (c_y, c_z))
    z_at = lax.rem(iota(shape, 0), 4)
    first_z, last_z = z_at == 0, z_at == 3
    step_x = jnp.where(falling, 1, -1)

    def rows(x, pair):
        done = []
        for rank in (2 * pair, 2 * pair + 1):
            y = Y_ORDER[rank]
            f = ext[x + 1, y + 1]
            flux = a_x * (f - ext[x + 1 + step_x, y + 1])
            flux = flux + a_y * (f - jnp.where(up_y, ext[x + 1, y], ext[x + 1, y + 2]))
            low = jnp.where(first_z, pltpu.roll(f, 5, 0), pltpu.roll(f, 1, 0))
            high = jnp.where(last_z, pltpu.roll(f, 3, 0), pltpu.roll(f, 7, 0))
            flux = flux + a_z * (f - jnp.where(up_z, low, high))
            read[x, rank] = f - flux
            done.append(f - flux)
        at = pl.multiple_of(32 * x + 16 * pair, 16)
        values[pl.ds(at, 16), :] = jnp.concatenate(done, axis=0).astype(BF16)

    hear(0)
    tell(1)
    first_inner = jnp.where(falling, 0, 1)

    def inner(k, _):
        rows(first_inner + k, 0)
        return 0

    lax.fori_loop(0, 7, inner, 0)
    hear(1)
    tell(2)

    for case in (True, False):

        @pl.when(even == case)
        def _():
            for copy in y_copies(case):
                copy.wait()

    outer_halo = jnp.where(even, 5, 0)
    for k, (first, width) in enumerate(SEGMENTS):
        y = 5 - outer_halo if k == 2 else outer_halo
        ext[1:9, y, :, first : first + width] = halo[k, :, 0:width].astype(F32).reshape(8, 8, width)

    for case in (True, False):

        @pl.when(falling == case)
        def _():
            x_copy(case).wait()

    edge = edge_in[...].astype(F32).reshape(4, 4, LOCAL)
    ext[9, 1:5, 4:8] = edge
    ext[0, 1:5, 0:4] = edge

    rows(jnp.where(falling, 7, 0), 0)

    def outer(x, _):
        rows(x, 1)
        return 0

    lax.fori_loop(0, 8, outer, 0)
    def block(ref, turn, device):
        return ref.at[turn, device // 2, pl.ds(pl.multiple_of(CELLS * lax.rem(device, 2), CELLS), CELLS)]

    def by_place(ref, turn, device):
        chip = device // 2
        rows = pl.ds(pl.multiple_of(CELLS * lax.rem(chip, 2), CELLS), CELLS)
        return ref.at[turn, lax.rem(device, 2), chip // 2, rows]

    def onward(turn, d):
        there = partner(d)
        return remote(
            block(send, turn, there), by_place(recv, turn, me),
            send_sem.at[turn, there], recv_sem.at[turn, me], {"vel": there},
        )

    def onward_from(turn, d):
        there = partner(d)
        return remote(
            block(send, turn, there), by_place(recv, turn, there),
            send_sem.at[turn, there], recv_sem.at[turn, there], {"vel": there},
        )

    def homeward(turn, d):
        there = partner(d)
        return remote(
            by_place(back, turn, there), block(packed, turn, me),
            back_send.at[turn, there], back_recv.at[turn, me], {"vel": there},
        )

    def homeward_from(turn, d):
        there = partner(d)
        return remote(
            by_place(back, turn, there), block(packed, turn, there),
            back_send.at[turn, there], back_recv.at[turn, there], {"vel": there},
        )

    for turn in range(TURNS):
        chosen = dot(picker[64 * turn : 64 * turn + 64], values[...]).astype(BF16)
        send[turn] = chosen.reshape(GROUPS // 2, 2 * CELLS, LOCAL)
        if turn == 0:
            hear(2)
        for d in order:
            onward(turn, d).start()
        own = pltpu.make_async_copy(
            block(send, turn, me), by_place(recv, turn, me), send_sem.at[turn, me]
        )
        own.start()

    for load in table_loads:
        load.wait()

    for b in range(NV):
        spread[:, NV * b : NV * b + NV] = raw[pl.ds(b, 3 * NV, stride=NV), :]
    high = spread[...].astype(BF16)
    parts = jnp.concatenate([high, (spread[...] - high.astype(F32)).astype(BF16)], axis=0)
    at = iota((6 * NV, 6 * NV), 0)
    a_at = lax.rem(at, NV)
    turn = (iota((6 * NV, 6 * NV), 1) == at - a_at + lax.rem(NV - a_at, NV)).astype(F32).astype(BF16)
    turned = dot(turn, parts).astype(BF16)
    lane_b, lane_c = iota((1, FREQ), 1) // NC, lax.rem(iota((1, FREQ), 1), NC)
    used = lane_c <= NV // 2
    same = jnp.where(used, lane_b * NV + lane_c, -1)
    other = jnp.where(used, lax.rem(NV - lane_b, NV) * NV + lax.rem(NV - lane_c, NV), -1)
    pick = iota((PLANE, FREQ), 0)
    both = dot(parts, (pick == same).astype(F32).astype(BF16)) + dot(
        turned, (pick == other).astype(F32).astype(BF16)
    )
    sym[...] = (both[: 3 * NV] + both[3 * NV :]) * (0.5 / float(NV**3))

    for turn in range(TURNS):
        pltpu.make_async_copy(
            block(send, turn, me), by_place(recv, turn, me), send_sem.at[turn, me]
        ).wait()
        for d in order:
            onward_from(turn, d).wait_recv()
        left, right = (recv[turn, core].reshape(CHIPS * CELLS, LOCAL).astype(F32) for core in range(2))
        cells = jnp.concatenate(
            [
                left[:, :PLANE],
                jnp.concatenate([left[:, PLANE:], right[:, :HALF]], axis=1),
                right[:, HALF:],
            ],
            axis=0,
        )
        section = dot(cells.astype(BF16), forward[...]).astype(BF16)
        turned = dot(into_x[...], section)
        spec_re = turned[:ROWS, :FREQ] + turned[ROWS:, FREQ:]
        spec_im = turned[:ROWS, FREQ:] - turned[ROWS:, :FREQ]
        spectra = []
        for k in range(3):
            weights = sym[k * NV : (k + 1) * NV]
            weights = jnp.concatenate([weights] * CELLS, axis=0)
            weighted = jnp.concatenate([spec_re * weights, spec_im * weights], axis=1).astype(BF16)
            turned = dot(from_x[...], weighted)
            spectra.append(
                jnp.concatenate(
                    [
                        turned[:ROWS, :FREQ] - turned[ROWS:, FREQ:],
                        turned[:ROWS, FREQ:] + turned[ROWS:, :FREQ],
                    ],
                    axis=1,
                ).astype(BF16)
            )
        filtered = dot(jnp.concatenate(spectra, axis=0), inverse[...])
        terms = filtered[:ROWS] * filtered[ROWS : 2 * ROWS] - cells * filtered[2 * ROWS :]
        third = CHIPS * CELLS
        low, middle, high = (terms[third * q : third * q + third] for q in range(3))
        back[turn, 0] = jnp.concatenate([low, middle[:, :HALF]], axis=1).astype(BF16).reshape(
            CHIPS // 2, 2 * CELLS, LOCAL
        )
        back[turn, 1] = jnp.concatenate([middle[:, HALF:], high], axis=1).astype(BF16).reshape(
            CHIPS // 2, 2 * CELLS, LOCAL
        )
        for d in order:
            homeward(turn, d).start()
        pltpu.make_async_copy(
            by_place(back, turn, me), block(packed, turn, me), back_send.at[turn, me]
        ).start()

    for turn in range(TURNS):
        pltpu.make_async_copy(
            by_place(back, turn, me), block(packed, turn, me), back_send.at[turn, me]
        ).wait()
        for d in order:
            homeward_from(turn, d).wait_recv()

    rates = lax.dot_general(
        placer, packed[...].reshape(TURNS * GROUPS * CELLS, LOCAL), (((0,), (0,)), ((), ())),
        preferred_element_type=F32,
    )
    evolved = read[...] + rates.reshape(8, 4, 8, LOCAL)
    for part in range(2):
        for rank, y in enumerate(Y_ORDER):
            out[8 * part : 8 * part + 8, y] = evolved[:, rank, 4 * part : 4 * part + 4]
    for turn in range(TURNS):
        for d in order:
            onward(turn, d).wait_send()
            homeward(turn, d).wait_send()


def in_hbm(array):
    return pltpu.with_memory_space_constraint(array, pltpu.MemorySpace.HBM)


def per_device(distribution, refine_level, gain_one, gain_two, loss_kernel):
    constants = tables()
    kernels = [k.reshape(PLANE, NV) for k in (gain_one, gain_two, loss_kernel)]
    hbm = pl.BlockSpec(memory_space=pltpu.MemorySpace.HBM)
    vmem = pl.BlockSpec(memory_space=pltpu.VMEM)
    dma = pltpu.SemaphoreType.DMA
    return pl.pallas_call(
        kernel,
        out_shape=pltpu.VMEM(distribution.shape, F32),
        in_specs=[hbm] * 9,
        out_specs=vmem,
        scratch_shapes=[
            pltpu.VMEM((10, 6, 8, LOCAL), F32),
            pltpu.VMEM((3, 64, SEG), BF16),
            pltpu.VMEM((3, 64, SEG), BF16),
            pltpu.VMEM((16, LOCAL), BF16),
            pltpu.VMEM((16, LOCAL), BF16),
            pltpu.VMEM((8, 4, 8, LOCAL), F32),
            pltpu.VMEM((256, LOCAL), BF16),
            pltpu.VMEM((TURNS, GROUPS // 2, 2 * CELLS, LOCAL), BF16),
            pltpu.VMEM((TURNS, 2, CHIPS // 2, 2 * CELLS, LOCAL), BF16),
            pltpu.VMEM((TURNS, 2, CHIPS // 2, 2 * CELLS, LOCAL), BF16),
            pltpu.VMEM((TURNS, GROUPS // 2, 2 * CELLS, LOCAL), BF16),
            pltpu.VMEM((PLANE, 2 * FREQ), BF16),
            pltpu.VMEM((2 * FREQ, PLANE), BF16),
            pltpu.VMEM((2 * ROWS, ROWS), BF16),
            pltpu.VMEM((2 * ROWS, ROWS), BF16),
            pltpu.VMEM((3 * PLANE, NV), F32),
            pltpu.VMEM((3 * NV, PLANE), F32),
            pltpu.VMEM((3 * NV, FREQ), F32),
            pltpu.VMEM((4, 4, 16), jnp.int32),
            dma((11,)), dma((7,)), pltpu.SemaphoreType.REGULAR((6,)), dma((3,)), dma((3,)),
            *[dma((TURNS, GROUPS))] * 4,
        ],
        compiler_params=pltpu.CompilerParams(
            collective_id=0, has_side_effects=True, vmem_limit_bytes=48 << 20
        ),
    )(*map(in_hbm, (distribution, refine_level.transpose(1, 2, 0), *kernels, *constants)))


def solution(mesh):
    in_specs = (P("cx", "cy", None, "vel"), P("cx", "cy", None), P(), P(), P())
    return jax.shard_map(
        per_device, mesh=mesh, in_specs=in_specs,
        out_specs=P("cx", "cy", None, "vel"), check_vma=False,
    )
```

```python
import functools
import math

import jax
import jax.numpy as jnp
import numpy as np
from jax import lax
from jax.experimental import pallas as pl
from jax.experimental.pallas import tpu as pltpu
from jax.sharding import PartitionSpec as P

MESH = pl.DeviceIdType.MESH
F32, BF16 = jnp.float32, jnp.bfloat16
NV, NC = 24, 16
PLANE, HALF, LOCAL = NV * NV, NV * NV // 2, NV * NV * 3 // 2
FREQ = NV * NC
GROUPS, CHIPS, CELLS, TURNS = 16, 8, 4, 2
ROWS = NV * CELLS
SEGMENTS = ((0, 384), (512, 352), (256, 384))
SEG = 384
Y_ORDER = (1, 2, 0, 3)


def tables():
    jk = np.arange(PLANE)
    bc = np.arange(FREQ)
    turns = (np.outer(jk // NV, bc // NC) + np.outer(jk % NV, bc % NC)) % NV
    keep = (bc % NC <= NV // 2).astype(np.float64)
    twice = np.where((bc % NC == 0) | (bc % NC == NV // 2), 1.0, 2.0) * keep
    cosine = np.round(np.cos(2 * np.pi * turns / NV), 12)
    sine = np.round(np.sin(2 * np.pi * turns / NV), 12)
    forward = np.concatenate([cosine * keep, -sine * keep], 1)
    inverse = np.concatenate([(cosine * twice).T, (-sine * twice).T], 0)
    row = np.arange(ROWS)
    i_at, i_cell = 3 * (row // CELLS % CHIPS) + row // (CELLS * CHIPS), row % CELLS
    a_at, a_cell = row % NV, row // NV
    turns = np.outer(a_at, i_at) % NV
    same = a_cell[:, None] == i_cell[None, :]
    cosine = np.round(np.cos(2 * np.pi * turns / NV), 12) * same
    sine = np.round(np.sin(2 * np.pi * turns / NV), 12) * same
    into_x = np.concatenate([cosine, sine], 0)
    from_x = np.concatenate([cosine.T, sine.T], 0)
    return tuple(jnp.asarray(t, dtype=BF16) for t in (forward, inverse, into_x, from_x))


def iota(shape, dim):
    return lax.broadcasted_iota(jnp.int32, shape, dim)


def dot(a, b):
    return jnp.dot(a, b, preferred_element_type=F32)


def kernel(
    dist, level_hbm, kernel_a, kernel_b, kernel_c, forward_hbm, inverse_hbm, into_hbm, from_hbm, out,
    ext, face, halo, edge_out, edge_in, read, values, send, recv, back, packed, forward, inverse, into_x, from_x, raw, spread, sym, level,
    local_sem, table_sem, hop_sem, face_send, face_recv, send_sem, recv_sem, back_send, back_recv,
):
    me = lax.axis_index("vel")
    my_x, my_y = lax.axis_index("cx"), lax.axis_index("cy")
    nx, ny = lax.axis_size("cx"), lax.axis_size("cy")
    x_low, x_high = {"cx": lax.rem(my_x + nx - 1, nx)}, {"cx": lax.rem(my_x + 1, nx)}
    y_low, y_high = {"cy": lax.rem(my_y + ny - 1, ny)}, {"cy": lax.rem(my_y + 1, ny)}
    falling = me < GROUPS // 2
    even = lax.rem(me, 2) == 0

    barrier = pltpu.get_barrier_semaphore()
    twin = me + 1 - 2 * lax.rem(me, 2)
    near = [twin] + [lax.rem(m + d, GROUPS) for m in (me, twin) for d in (2, GROUPS - 2)]
    beside = [x_low, x_high, y_low, y_high] + [{"vel": v} for v in near]
    for there in beside:
        pl.semaphore_signal(barrier, inc=1, device_id=there, device_id_type=MESH)
    loads = [
        pltpu.make_async_copy(
            dist.at[8 * s : 8 * s + 8, y], ext.at[1:9, y + 1, 4 * s : 4 * s + 4], local_sem.at[2 * y + s]
        )
        for y in (0, 3, 1, 2)
        for s in range(2)
    ]
    loads += [
        pltpu.make_async_copy(dist.at[8], ext.at[9, 1:5, 0:4], local_sem.at[8]),
        pltpu.make_async_copy(dist.at[7], ext.at[0, 1:5, 4:8], local_sem.at[9]),
        pltpu.make_async_copy(level_hbm, level, local_sem.at[10]),
    ]
    for load in loads:
        load.start()
    table_loads = [
        pltpu.make_async_copy(src, dst, table_sem.at[k])
        for k, (src, dst) in enumerate(
            (
                (forward_hbm, forward), (inverse_hbm, inverse), (into_hbm, into_x), (from_hbm, from_x),
                (kernel_a, raw.at[0:PLANE]), (kernel_b, raw.at[PLANE : 2 * PLANE]),
                (kernel_c, raw.at[2 * PLANE : 3 * PLANE]),
            )
        )
    ]

    order = [(dz, t) for dz in (4, 3, -3, 2, -2, 1, -1, 0) for t in (0, 1) if (dz, t) != (0, 0)]

    def partner(d):
        return lax.rem((twin if d[1] else me) + 2 * d[0] + GROUPS, GROUPS)


    def remote(src, dst, send_at, recv_at, there):
        return pltpu.make_async_remote_copy(
            src_ref=src, dst_ref=dst, send_sem=send_at, recv_sem=recv_at,
            device_id=there, device_id_type=MESH,
        )

    def x_copy(up):
        return remote(edge_out, edge_in, face_send.at[0], face_recv.at[0], x_low if up else x_high)

    def y_copies(is_even):
        outer = remote(
            face.at[0:2], halo.at[0:2], face_send.at[1], face_recv.at[1],
            y_low if is_even else y_high,
        )
        middle = remote(
            face.at[2], halo.at[2], face_send.at[2], face_recv.at[2],
            y_high if is_even else y_low,
        )
        return outer, middle

    for load in loads[:4]:
        load.wait()
    outer_y = jnp.where(even, 1, 4)
    for k, (first, width) in enumerate(SEGMENTS):
        y = 5 - outer_y if k == 2 else outer_y
        face[k, :, 0:width] = ext[1:9, y, :, first : first + width].reshape(64, width).astype(BF16)

    for load in loads[4:]:
        load.wait()
    edge = jnp.where(falling, ext[1, 1:5, 0:4], ext[8, 1:5, 4:8])
    edge_out[...] = edge.reshape(16, LOCAL).astype(BF16)

    pl.semaphore_wait(barrier, len(beside))
    for case in (True, False):

        @pl.when(even == case)
        def _():
            for copy in y_copies(case):
                copy.start()

    for case in (True, False):

        @pl.when(falling == case)
        def _():
            x_copy(case).start()

    for load in table_loads:
        load.start()
    def tell(k):
        for side, d in enumerate((2, GROUPS - 2)):
            pl.semaphore_signal(
                hop_sem.at[2 * k + side], inc=1, device_id={"vel": lax.rem(me + d, GROUPS)},
                device_id_type=MESH,
            )

    def hear(k):
        for side in range(2):
            pl.semaphore_wait(hop_sem.at[2 * k + side], 1)

    tell(0)

    levels = jnp.concatenate([level[y] for y in range(4)], axis=0).astype(F32).astype(BF16)
    r = iota((16, 256), 1)
    row = iota((16, 256), 0)
    x_hot = (row == lax.rem(r // 4, 2) * 8 + r // 32).astype(F32).astype(BF16)
    y_rank = lax.rem(r // 8, 4)
    yz_hot = row == jnp.where(y_rank < 2, y_rank + 1, 3 * y_rank - 6) * 4 + lax.rem(r, 4)
    by_yz = dot(levels, x_hot)
    level_row = jnp.sum(jnp.where(yz_hot, by_yz, 0.0), axis=0, keepdims=True)
    active = (level_row > 0.5).astype(F32)
    upto = (iota((256, 256), 0) <= iota((256, 256), 1)).astype(F32).astype(BF16)
    slot = dot(jnp.broadcast_to(active, (8, 256)).astype(BF16), upto)[0:1] - 1.0
    hot = (
        (iota((128, 256), 0).astype(F32) == slot) & (jnp.broadcast_to(active, (128, 256)) > 0.5)
    ).astype(F32)
    picker = hot.astype(BF16)
    placer = (hot * (0.25 * level_row)).astype(BF16)

    lane = iota((1, LOCAL), 1) + me * LOCAL

    def speed(index):
        return 0.3 * (2.0 * index.astype(F32) - (NV - 1)) / (NV - 1)

    c_x = speed(lane // PLANE)
    c_y = speed(lax.rem(lane // NV, NV))
    c_z = speed(lax.rem(lane, NV))
    shape = (8, LOCAL)
    a_x, a_y, a_z = (jnp.broadcast_to(jnp.abs(c), shape) for c in (c_x, c_y, c_z))
    up_y, up_z = (jnp.broadcast_to(c, shape) > 0.0 for c in (c_y, c_z))
    z_at = lax.rem(iota(shape, 0), 4)
    first_z, last_z = z_at == 0, z_at == 3
    step_x = jnp.where(falling, 1, -1)

    def rows(x, pair):
        done = []
        for rank in (2 * pair, 2 * pair + 1):
            y = Y_ORDER[rank]
            f = ext[x + 1, y + 1]
            flux = a_x * (f - ext[x + 1 + step_x, y + 1])
            flux = flux + a_y * (f - jnp.where(up_y, ext[x + 1, y], ext[x + 1, y + 2]))
            low = jnp.where(first_z, pltpu.roll(f, 5, 0), pltpu.roll(f, 1, 0))
            high = jnp.where(last_z, pltpu.roll(f, 3, 0), pltpu.roll(f, 7, 0))
            flux = flux + a_z * (f - jnp.where(up_z, low, high))
            read[x, rank] = f - flux
            done.append(f - flux)
        at = pl.multiple_of(32 * x + 16 * pair, 16)
        values[pl.ds(at, 16), :] = jnp.concatenate(done, axis=0).astype(BF16)

    hear(0)
    tell(1)
    first_inner = jnp.where(falling, 0, 1)

    def inner(k, _):
        rows(first_inner + k, 0)
        return 0

    lax.fori_loop(0, 7, inner, 0)
    hear(1)
    tell(2)

    for case in (True, False):

        @pl.when(even == case)
        def _():
            for copy in y_copies(case):
                copy.wait()

    outer_halo = jnp.where(even, 5, 0)
    for k, (first, width) in enumerate(SEGMENTS):
        y = 5 - outer_halo if k == 2 else outer_halo
        ext[1:9, y, :, first : first + width] = halo[k, :, 0:width].astype(F32).reshape(8, 8, width)

    for case in (True, False):

        @pl.when(falling == case)
        def _():
            x_copy(case).wait()

    edge = edge_in[...].astype(F32).reshape(4, 4, LOCAL)
    ext[9, 1:5, 4:8] = edge
    ext[0, 1:5, 0:4] = edge

    rows(jnp.where(falling, 7, 0), 0)

    def outer(x, _):
        rows(x, 1)
        return 0

    lax.fori_loop(0, 8, outer, 0)
    def by_place(ref, turn, device):
        return ref.at[turn, lax.rem(device, 2), device // 2]

    def onward(turn, d):
        there = partner(d)
        return remote(
            send.at[turn, there], by_place(recv, turn, me), send_sem.at[turn], recv_sem.at[turn],
            {"vel": there},
        )

    def homeward(turn, d):
        there = partner(d)
        return remote(
            by_place(back, turn, there), packed.at[turn, me], back_send.at[turn], back_recv.at[turn],
            {"vel": there},
        )

    def all_of(ref, turn, sem):
        pltpu.make_async_copy(ref.at[turn], ref.at[turn], sem.at[turn]).wait()

    def others_of(ref, turn, sem):
        pltpu.make_async_copy(
            ref.at[turn, 0 : GROUPS - 1], ref.at[turn, 0 : GROUPS - 1], sem.at[turn]
        ).wait()

    for turn in range(TURNS):
        chosen = dot(picker[64 * turn : 64 * turn + 64], values[...])
        send[turn] = chosen.reshape(GROUPS, CELLS, LOCAL).astype(BF16)
        if turn == 0:
            hear(2)
        for d in order:
            onward(turn, d).start()
        pltpu.make_async_copy(send.at[turn, me], by_place(recv, turn, me), recv_sem.at[turn]).start()

    for load in table_loads:
        load.wait()

    for b in range(NV):
        spread[:, NV * b : NV * b + NV] = raw[pl.ds(b, 3 * NV, stride=NV), :]
    high = spread[...].astype(BF16)
    parts = jnp.concatenate([high, (spread[...] - high.astype(F32)).astype(BF16)], axis=0)
    at = iota((6 * NV, 6 * NV), 0)
    a_at = lax.rem(at, NV)
    turn = (iota((6 * NV, 6 * NV), 1) == at - a_at + lax.rem(NV - a_at, NV)).astype(F32).astype(BF16)
    turned = dot(turn, parts).astype(BF16)
    lane_b, lane_c = iota((1, FREQ), 1) // NC, lax.rem(iota((1, FREQ), 1), NC)
    used = lane_c <= NV // 2
    same = jnp.where(used, lane_b * NV + lane_c, -1)
    other = jnp.where(used, lax.rem(NV - lane_b, NV) * NV + lax.rem(NV - lane_c, NV), -1)
    pick = iota((PLANE, FREQ), 0)
    both = dot(parts, (pick == same).astype(F32).astype(BF16)) + dot(
        turned, (pick == other).astype(F32).astype(BF16)
    )
    sym[...] = (both[: 3 * NV] + both[3 * NV :]) * (0.5 / float(NV**3))

    for turn in range(TURNS):
        all_of(recv, turn, recv_sem)
        left, right = (
            recv[turn, core].astype(F32).reshape(CHIPS * CELLS, LOCAL) for core in range(2)
        )
        cells = jnp.concatenate(
            [
                left[:, :PLANE],
                jnp.concatenate([left[:, PLANE:], right[:, :HALF]], axis=1),
                right[:, HALF:],
            ],
            axis=0,
        )
        section = dot(cells.astype(BF16), forward[...]).astype(BF16)
        turned = dot(into_x[...], section)
        spec_re = turned[:ROWS, :FREQ] + turned[ROWS:, FREQ:]
        spec_im = turned[:ROWS, FREQ:] - turned[ROWS:, :FREQ]
        spectra = []
        for k in range(3):
            weights = sym[k * NV : (k + 1) * NV]
            weights = jnp.concatenate([weights] * CELLS, axis=0)
            weighted = jnp.concatenate([spec_re * weights, spec_im * weights], axis=1).astype(BF16)
            turned = dot(from_x[...], weighted)
            spectra.append(
                jnp.concatenate(
                    [
                        turned[:ROWS, :FREQ] - turned[ROWS:, FREQ:],
                        turned[:ROWS, FREQ:] + turned[ROWS:, :FREQ],
                    ],
                    axis=1,
                ).astype(BF16)
            )
        filtered = dot(jnp.concatenate(spectra, axis=0), inverse[...])
        terms = filtered[:ROWS] * filtered[ROWS : 2 * ROWS] - cells * filtered[2 * ROWS :]
        third = CHIPS * CELLS
        low, middle, high = (terms[third * q : third * q + third] for q in range(3))
        sides = (
            jnp.concatenate([low, middle[:, :HALF]], axis=1),
            jnp.concatenate([middle[:, HALF:], high], axis=1),
        )
        for core in range(2):
            back[turn, core] = sides[core].reshape(CHIPS, CELLS, LOCAL).astype(BF16)
        for d in order:
            homeward(turn, d).start()
        pltpu.make_async_copy(
            by_place(back, turn, me), packed.at[turn, me], back_recv.at[turn]
        ).start()

    for turn in range(TURNS):
        all_of(packed, turn, back_recv)
        rates = lax.dot_general(
            placer[64 * turn : 64 * turn + 64],
            packed[turn].astype(F32).reshape(GROUPS * CELLS, LOCAL).astype(BF16),
            (((0,), (0,)), ((), ())), preferred_element_type=F32,
        )
        evolved = read[...] + rates.reshape(8, 4, 8, LOCAL)
        if turn < TURNS - 1:
            read[...] = evolved
    for part in range(2):
        for rank, y in enumerate(Y_ORDER):
            out[8 * part : 8 * part + 8, y] = evolved[:, rank, 4 * part : 4 * part + 4]
    for turn in range(TURNS):
        others_of(send, turn, send_sem)
        others_of(packed, turn, back_send)


def in_hbm(array):
    return pltpu.with_memory_space_constraint(array, pltpu.MemorySpace.HBM)


def per_device(distribution, refine_level, gain_one, gain_two, loss_kernel):
    constants = tables()
    kernels = [k.reshape(PLANE, NV) for k in (gain_one, gain_two, loss_kernel)]
    hbm = pl.BlockSpec(memory_space=pltpu.MemorySpace.HBM)
    vmem = pl.BlockSpec(memory_space=pltpu.VMEM)
    dma = pltpu.SemaphoreType.DMA
    return pl.pallas_call(
        kernel,
        out_shape=pltpu.VMEM(distribution.shape, F32),
        in_specs=[hbm] * 9,
        out_specs=vmem,
        scratch_shapes=[
            pltpu.VMEM((10, 6, 8, LOCAL), F32),
            pltpu.VMEM((3, 64, SEG), BF16),
            pltpu.VMEM((3, 64, SEG), BF16),
            pltpu.VMEM((16, LOCAL), BF16),
            pltpu.VMEM((16, LOCAL), BF16),
            pltpu.VMEM((8, 4, 8, LOCAL), F32),
            pltpu.VMEM((256, LOCAL), BF16),
            pltpu.VMEM((TURNS, GROUPS, CELLS, LOCAL), BF16),
            pltpu.VMEM((TURNS, 2, CHIPS, CELLS, LOCAL), BF16),
            pltpu.VMEM((TURNS, 2, CHIPS, CELLS, LOCAL), BF16),
            pltpu.VMEM((TURNS, GROUPS, CELLS, LOCAL), BF16),
            pltpu.VMEM((PLANE, 2 * FREQ), BF16),
            pltpu.VMEM((2 * FREQ, PLANE), BF16),
            pltpu.VMEM((2 * ROWS, ROWS), BF16),
            pltpu.VMEM((2 * ROWS, ROWS), BF16),
            pltpu.VMEM((3 * PLANE, NV), F32),
            pltpu.VMEM((3 * NV, PLANE), F32),
            pltpu.VMEM((3 * NV, FREQ), F32),
            pltpu.VMEM((4, 4, 16), jnp.int32),
            dma((11,)), dma((7,)), pltpu.SemaphoreType.REGULAR((6,)), dma((3,)), dma((3,)),
            *[dma((TURNS,))] * 4,
        ],
        compiler_params=pltpu.CompilerParams(
            collective_id=0, has_side_effects=True, vmem_limit_bytes=48 << 20
        ),
    )(*map(in_hbm, (distribution, refine_level.transpose(1, 2, 0), *kernels, *constants)))


def solution(mesh):
    in_specs = (P("cx", "cy", None, "vel"), P("cx", "cy", None), P(), P(), P())
    return jax.shard_map(
        per_device, mesh=mesh, in_specs=in_specs,
        out_specs=P("cx", "cy", None, "vel"), check_vma=False,
    )
```

```python
import functools
import math

import jax
import jax.numpy as jnp
import numpy as np
from jax import lax
from jax.experimental import pallas as pl
from jax.experimental.pallas import tpu as pltpu
from jax.sharding import PartitionSpec as P

MESH = pl.DeviceIdType.MESH
F32, BF16 = jnp.float32, jnp.bfloat16
NV, NC = 24, 16
PLANE, HALF, LOCAL = NV * NV, NV * NV // 2, NV * NV * 3 // 2
FREQ = NV * NC
GROUPS, CHIPS, CELLS, TURNS = 16, 8, 2, 4
SLOTS = GROUPS * CELLS
ROWS = NV * CELLS
SEGMENTS = ((0, 384), (512, 352), (256, 384))
SEG = 384
Y_ORDER = (1, 2, 0, 3)


def tables():
    jk = np.arange(PLANE)
    bc = np.arange(FREQ)
    turns = (np.outer(jk // NV, bc // NC) + np.outer(jk % NV, bc % NC)) % NV
    keep = (bc % NC <= NV // 2).astype(np.float64)
    twice = np.where((bc % NC == 0) | (bc % NC == NV // 2), 1.0, 2.0) * keep
    cosine = np.round(np.cos(2 * np.pi * turns / NV), 12)
    sine = np.round(np.sin(2 * np.pi * turns / NV), 12)
    forward = np.concatenate([cosine * keep, -sine * keep], 1)
    inverse = np.concatenate([(cosine * twice).T, (-sine * twice).T], 0)
    row = np.arange(ROWS)
    i_at, i_cell = 3 * (row // CELLS % CHIPS) + row // (CELLS * CHIPS), row % CELLS
    a_at, a_cell = row % NV, row // NV
    turns = np.outer(a_at, i_at) % NV
    same = a_cell[:, None] == i_cell[None, :]
    cosine = np.round(np.cos(2 * np.pi * turns / NV), 12) * same
    sine = np.round(np.sin(2 * np.pi * turns / NV), 12) * same
    into_x = np.concatenate([cosine, sine], 0)
    from_x = np.concatenate([cosine.T, sine.T], 0)
    return tuple(jnp.asarray(t, dtype=BF16) for t in (forward, inverse, into_x, from_x))


def iota(shape, dim):
    return lax.broadcasted_iota(jnp.int32, shape, dim)


def dot(a, b):
    return jnp.dot(a, b, preferred_element_type=F32)


def kernel(
    dist, level_hbm, kernel_a, kernel_b, kernel_c, forward_hbm, inverse_hbm, into_hbm, from_hbm, out,
    ext, face, halo, edge_out, edge_in, read, values, send, recv, back, packed, forward, inverse, into_x, from_x, raw, spread, sym, level,
    local_sem, table_sem, hop_sem, face_send, face_recv, send_sem, recv_sem, back_send, back_recv,
):
    me = lax.axis_index("vel")
    my_x, my_y = lax.axis_index("cx"), lax.axis_index("cy")
    nx, ny = lax.axis_size("cx"), lax.axis_size("cy")
    x_low, x_high = {"cx": lax.rem(my_x + nx - 1, nx)}, {"cx": lax.rem(my_x + 1, nx)}
    y_low, y_high = {"cy": lax.rem(my_y + ny - 1, ny)}, {"cy": lax.rem(my_y + 1, ny)}
    falling = me < GROUPS // 2
    even = lax.rem(me, 2) == 0

    barrier = pltpu.get_barrier_semaphore()
    twin = me + 1 - 2 * lax.rem(me, 2)
    near = [twin] + [lax.rem(m + d, GROUPS) for m in (me, twin) for d in (2, GROUPS - 2)]
    beside = [x_low, x_high, y_low, y_high] + [{"vel": v} for v in near]
    for there in beside:
        pl.semaphore_signal(barrier, inc=1, device_id=there, device_id_type=MESH)
    loads = [
        pltpu.make_async_copy(
            dist.at[8 * s : 8 * s + 8], ext.at[1:9, 1:5, 4 * s : 4 * s + 4], local_sem.at[s]
        )
        for s in range(2)
    ]
    loads += [
        pltpu.make_async_copy(dist.at[8], ext.at[9, 1:5, 0:4], local_sem.at[2]),
        pltpu.make_async_copy(dist.at[7], ext.at[0, 1:5, 4:8], local_sem.at[3]),
        pltpu.make_async_copy(level_hbm, level, local_sem.at[4]),
    ]
    for load in loads:
        load.start()
    table_loads = [
        pltpu.make_async_copy(src, dst, table_sem.at[k])
        for k, (src, dst) in enumerate(
            (
                (forward_hbm, forward), (inverse_hbm, inverse), (into_hbm, into_x), (from_hbm, from_x),
                (kernel_a, raw.at[0:PLANE]), (kernel_b, raw.at[PLANE : 2 * PLANE]),
                (kernel_c, raw.at[2 * PLANE : 3 * PLANE]),
            )
        )
    ]

    order = [(dz, t) for dz in (4, 3, -3, 2, -2, 1, -1, 0) for t in (0, 1) if (dz, t) != (0, 0)]

    def partner(d):
        return lax.rem((twin if d[1] else me) + 2 * d[0] + GROUPS, GROUPS)


    def remote(src, dst, send_at, recv_at, there):
        return pltpu.make_async_remote_copy(
            src_ref=src, dst_ref=dst, send_sem=send_at, recv_sem=recv_at,
            device_id=there, device_id_type=MESH,
        )

    def x_copy(up):
        return remote(edge_out, edge_in, face_send.at[0], face_recv.at[0], x_low if up else x_high)

    def y_copies(is_even):
        outer = remote(
            face.at[0:2], halo.at[0:2], face_send.at[1], face_recv.at[1],
            y_low if is_even else y_high,
        )
        middle = remote(
            face.at[2], halo.at[2], face_send.at[2], face_recv.at[2],
            y_high if is_even else y_low,
        )
        return outer, middle

    for load in loads[:2]:
        load.wait()
    outer_y = jnp.where(even, 1, 4)
    for k, (first, width) in enumerate(SEGMENTS):
        y = 5 - outer_y if k == 2 else outer_y
        face[k, :, 0:width] = ext[1:9, y, :, first : first + width].reshape(64, width).astype(BF16)

    for load in loads[2:]:
        load.wait()
    edge = jnp.where(falling, ext[1, 1:5, 0:4], ext[8, 1:5, 4:8])
    edge_out[...] = edge.reshape(16, LOCAL).astype(BF16)

    pl.semaphore_wait(barrier, len(beside))
    for case in (True, False):

        @pl.when(even == case)
        def _():
            for copy in y_copies(case):
                copy.start()

    for case in (True, False):

        @pl.when(falling == case)
        def _():
            x_copy(case).start()

    for load in table_loads:
        load.start()
    def tell(k):
        for side, d in enumerate((2, GROUPS - 2)):
            pl.semaphore_signal(
                hop_sem.at[2 * k + side], inc=1, device_id={"vel": lax.rem(me + d, GROUPS)},
                device_id_type=MESH,
            )

    def hear(k):
        for side in range(2):
            pl.semaphore_wait(hop_sem.at[2 * k + side], 1)

    tell(0)

    levels = jnp.concatenate([level[y] for y in range(4)], axis=0).astype(F32).astype(BF16)
    r = iota((16, 256), 1)
    row = iota((16, 256), 0)
    x_hot = (row == lax.rem(r // 4, 2) * 8 + r // 32).astype(F32).astype(BF16)
    y_rank = lax.rem(r // 8, 4)
    yz_hot = row == jnp.where(y_rank < 2, y_rank + 1, 3 * y_rank - 6) * 4 + lax.rem(r, 4)
    by_yz = dot(levels, x_hot)
    level_row = jnp.sum(jnp.where(yz_hot, by_yz, 0.0), axis=0, keepdims=True)
    active = (level_row > 0.5).astype(F32)
    upto = (iota((256, 256), 0) <= iota((256, 256), 1)).astype(F32).astype(BF16)
    slot = dot(jnp.broadcast_to(active, (8, 256)).astype(BF16), upto)[0:1] - 1.0
    hot = (
        (iota((128, 256), 0).astype(F32) == slot) & (jnp.broadcast_to(active, (128, 256)) > 0.5)
    ).astype(F32)
    picker = hot.astype(BF16)
    placer = (hot * (0.25 * level_row)).astype(BF16)

    lane = iota((1, LOCAL), 1) + me * LOCAL

    def speed(index):
        return 0.3 * (2.0 * index.astype(F32) - (NV - 1)) / (NV - 1)

    c_x = speed(lane // PLANE)
    c_y = speed(lax.rem(lane // NV, NV))
    c_z = speed(lax.rem(lane, NV))
    shape = (8, LOCAL)
    a_x, a_y, a_z = (jnp.broadcast_to(jnp.abs(c), shape) for c in (c_x, c_y, c_z))
    up_y, up_z = (jnp.broadcast_to(c, shape) > 0.0 for c in (c_y, c_z))
    z_at = lax.rem(iota(shape, 0), 4)
    first_z, last_z = z_at == 0, z_at == 3
    step_x = jnp.where(falling, 1, -1)

    def keep(x, pair, done):
        at = pl.multiple_of(32 * x + 16 * pair, 16)
        values[pl.ds(at, 16), :] = jnp.concatenate(done, axis=0).astype(BF16)

    def along_xz(x, y):
        f = ext[x + 1, y + 1]
        low = jnp.where(first_z, pltpu.roll(f, 5, 0), pltpu.roll(f, 1, 0))
        high = jnp.where(last_z, pltpu.roll(f, 3, 0), pltpu.roll(f, 7, 0))
        flux = a_x * (f - ext[x + 1 + step_x, y + 1])
        return f - (flux + a_z * (f - jnp.where(up_z, low, high)))

    def along_y(x, y):
        return a_y * (ext[x + 1, y + 1] - jnp.where(up_y, ext[x + 1, y], ext[x + 1, y + 2]))

    def before_halo(x):
        done = []
        for rank, y in enumerate(Y_ORDER):
            left = along_xz(x, y)
            if rank < 2:
                left = left - along_y(x, y)
                done.append(left)
            read[x, rank] = left
        keep(x, 0, done)

    first_inner = jnp.where(falling, 0, 1)

    def inner(k, _):
        before_halo(first_inner + k)
        return 0

    hear(0)
    tell(1)
    lax.fori_loop(0, 7, inner, 0)
    hear(1)
    tell(2)

    for case in (True, False):

        @pl.when(even == case)
        def _():
            for copy in y_copies(case):
                copy.wait()

    outer_halo = jnp.where(even, 5, 0)
    for k, (first, width) in enumerate(SEGMENTS):
        y = 5 - outer_halo if k == 2 else outer_halo
        ext[1:9, y, :, first : first + width] = halo[k, :, 0:width].astype(F32).reshape(8, 8, width)

    for case in (True, False):

        @pl.when(falling == case)
        def _():
            x_copy(case).wait()

    edge = edge_in[...].astype(F32).reshape(4, 4, LOCAL)
    ext[9, 1:5, 4:8] = edge
    ext[0, 1:5, 0:4] = edge

    before_halo(jnp.where(falling, 7, 0))

    def outer(x, _):
        done = []
        for rank in (2, 3):
            evolved = read[x, rank] - along_y(x, Y_ORDER[rank])
            read[x, rank] = evolved
            done.append(evolved)
        keep(x, 1, done)
        return 0

    lax.fori_loop(0, 8, outer, 0)

    def by_place(ref, turn, device):
        return ref.at[turn, lax.rem(device, 2), device // 2]

    def onward(turn, d):
        there = partner(d)
        return remote(
            send.at[turn, there], by_place(recv, turn, me), send_sem.at[turn], recv_sem.at[turn],
            {"vel": there},
        )

    def homeward(turn, d):
        there = partner(d)
        return remote(
            by_place(back, turn, there), packed.at[turn, me], back_send.at[turn], back_recv.at[turn],
            {"vel": there},
        )

    def all_of(ref, turn, sem):
        pltpu.make_async_copy(ref.at[turn], ref.at[turn], sem.at[turn]).wait()

    def others_of(ref, turn, sem):
        pltpu.make_async_copy(
            ref.at[turn, 0 : GROUPS - 1], ref.at[turn, 0 : GROUPS - 1], sem.at[turn]
        ).wait()

    for turn in range(TURNS):
        chosen = dot(picker[SLOTS * turn : SLOTS * (turn + 1)], values[...])
        send[turn] = chosen.reshape(GROUPS, CELLS, LOCAL).astype(BF16)
        if turn == 0:
            hear(2)
        for d in order:
            onward(turn, d).start()
        pltpu.make_async_copy(send.at[turn, me], by_place(recv, turn, me), recv_sem.at[turn]).start()

    for load in table_loads:
        load.wait()

    for b in range(NV):
        spread[:, NV * b : NV * b + NV] = raw[pl.ds(b, 3 * NV, stride=NV), :]
    high = spread[...].astype(BF16)
    parts = jnp.concatenate([high, (spread[...] - high.astype(F32)).astype(BF16)], axis=0)
    at = iota((6 * NV, 6 * NV), 0)
    a_at = lax.rem(at, NV)
    turn = (iota((6 * NV, 6 * NV), 1) == at - a_at + lax.rem(NV - a_at, NV)).astype(F32).astype(BF16)
    turned = dot(turn, parts).astype(BF16)
    lane_b, lane_c = iota((1, FREQ), 1) // NC, lax.rem(iota((1, FREQ), 1), NC)
    used = lane_c <= NV // 2
    same = jnp.where(used, lane_b * NV + lane_c, -1)
    other = jnp.where(used, lax.rem(NV - lane_b, NV) * NV + lax.rem(NV - lane_c, NV), -1)
    pick = iota((PLANE, FREQ), 0)
    both = dot(parts, (pick == same).astype(F32).astype(BF16)) + dot(
        turned, (pick == other).astype(F32).astype(BF16)
    )
    sym[...] = (both[: 3 * NV] + both[3 * NV :]) * (0.5 / float(NV**3))

    for turn in range(TURNS):
        all_of(recv, turn, recv_sem)
        left, right = (
            recv[turn, core].astype(F32).reshape(CHIPS * CELLS, LOCAL) for core in range(2)
        )
        cells = jnp.concatenate(
            [
                left[:, :PLANE],
                jnp.concatenate([left[:, PLANE:], right[:, :HALF]], axis=1),
                right[:, HALF:],
            ],
            axis=0,
        )
        section = dot(cells.astype(BF16), forward[...]).astype(BF16)
        turned = dot(into_x[...], section)
        spec_re = turned[:ROWS, :FREQ] + turned[ROWS:, FREQ:]
        spec_im = turned[:ROWS, FREQ:] - turned[ROWS:, :FREQ]
        spectra = []
        for k in range(3):
            weights = sym[k * NV : (k + 1) * NV]
            weights = jnp.concatenate([weights] * CELLS, axis=0)
            weighted = jnp.concatenate([spec_re * weights, spec_im * weights], axis=1).astype(BF16)
            turned = dot(from_x[...], weighted)
            spectra.append(
                jnp.concatenate(
                    [
                        turned[:ROWS, :FREQ] - turned[ROWS:, FREQ:],
                        turned[:ROWS, FREQ:] + turned[ROWS:, :FREQ],
                    ],
                    axis=1,
                ).astype(BF16)
            )
        filtered = dot(jnp.concatenate(spectra, axis=0), inverse[...])
        terms = filtered[:ROWS] * filtered[ROWS : 2 * ROWS] - cells * filtered[2 * ROWS :]
        third = CHIPS * CELLS
        low, middle, high = (terms[third * q : third * q + third] for q in range(3))
        sides = (
            jnp.concatenate([low, middle[:, :HALF]], axis=1),
            jnp.concatenate([middle[:, HALF:], high], axis=1),
        )
        for core in range(2):
            back[turn, core] = sides[core].reshape(CHIPS, CELLS, LOCAL).astype(BF16)
        for d in order:
            homeward(turn, d).start()
        pltpu.make_async_copy(
            by_place(back, turn, me), packed.at[turn, me], back_recv.at[turn]
        ).start()

    def rates(first, last):
        terms = [
            packed[turn].astype(F32).reshape(SLOTS, LOCAL).astype(BF16) for turn in range(first, last)
        ]
        given = lax.dot_general(
            placer[SLOTS * first : SLOTS * last], jnp.concatenate(terms, axis=0),
            (((0,), (0,)), ((), ())), preferred_element_type=F32,
        )
        return given.reshape(8, 4, 8, LOCAL)

    for turn in range(TURNS - 1):
        all_of(packed, turn, back_recv)
    read[...] = read[...] + rates(0, TURNS - 1)
    all_of(packed, TURNS - 1, back_recv)
    evolved = read[...] + rates(TURNS - 1, TURNS)
    for part in range(2):
        for rank, y in enumerate(Y_ORDER):
            out[8 * part : 8 * part + 8, y] = evolved[:, rank, 4 * part : 4 * part + 4]
    for turn in range(TURNS):
        others_of(send, turn, send_sem)
        others_of(packed, turn, back_send)


def in_hbm(array):
    return pltpu.with_memory_space_constraint(array, pltpu.MemorySpace.HBM)


def per_device(distribution, refine_level, gain_one, gain_two, loss_kernel):
    constants = tables()
    kernels = [k.reshape(PLANE, NV) for k in (gain_one, gain_two, loss_kernel)]
    hbm = pl.BlockSpec(memory_space=pltpu.MemorySpace.HBM)
    vmem = pl.BlockSpec(memory_space=pltpu.VMEM)
    dma = pltpu.SemaphoreType.DMA
    return pl.pallas_call(
        kernel,
        out_shape=pltpu.VMEM(distribution.shape, F32),
        in_specs=[hbm] * 9,
        out_specs=vmem,
        scratch_shapes=[
            pltpu.VMEM((10, 6, 8, LOCAL), F32),
            pltpu.VMEM((3, 64, SEG), BF16),
            pltpu.VMEM((3, 64, SEG), BF16),
            pltpu.VMEM((16, LOCAL), BF16),
            pltpu.VMEM((16, LOCAL), BF16),
            pltpu.VMEM((8, 4, 8, LOCAL), F32),
            pltpu.VMEM((256, LOCAL), BF16),
            pltpu.VMEM((TURNS, GROUPS, CELLS, LOCAL), BF16),
            pltpu.VMEM((TURNS, 2, CHIPS, CELLS, LOCAL), BF16),
            pltpu.VMEM((TURNS, 2, CHIPS, CELLS, LOCAL), BF16),
            pltpu.VMEM((TURNS, GROUPS, CELLS, LOCAL), BF16),
            pltpu.VMEM((PLANE, 2 * FREQ), BF16),
            pltpu.VMEM((2 * FREQ, PLANE), BF16),
            pltpu.VMEM((2 * ROWS, ROWS), BF16),
            pltpu.VMEM((2 * ROWS, ROWS), BF16),
            pltpu.VMEM((3 * PLANE, NV), F32),
            pltpu.VMEM((3 * NV, PLANE), F32),
            pltpu.VMEM((3 * NV, FREQ), F32),
            pltpu.VMEM((4, 4, 16), jnp.int32),
            dma((5,)), dma((7,)), pltpu.SemaphoreType.REGULAR((6,)), dma((3,)), dma((3,)),
            *[dma((TURNS,))] * 4,
        ],
        compiler_params=pltpu.CompilerParams(
            collective_id=0, has_side_effects=True, vmem_limit_bytes=48 << 20
        ),
    )(*map(in_hbm, (distribution, refine_level.transpose(1, 2, 0), *kernels, *constants)))


def solution(mesh):
    in_specs = (P("cx", "cy", None, "vel"), P("cx", "cy", None), P(), P(), P())
    return jax.shard_map(
        per_device, mesh=mesh, in_specs=in_specs,
        out_specs=P("cx", "cy", None, "vel"), check_vma=False,
    )
```

```python
import functools
import math

import jax
import jax.numpy as jnp
import numpy as np
from jax import lax
from jax.experimental import pallas as pl
from jax.experimental.pallas import tpu as pltpu
from jax.sharding import PartitionSpec as P

MESH = pl.DeviceIdType.MESH
F32, BF16 = jnp.float32, jnp.bfloat16
NV, NC = 24, 16
PLANE, HALF, LOCAL = NV * NV, NV * NV // 2, NV * NV * 3 // 2
FREQ = NV * NC
GROUPS, CHIPS, CELLS, TURNS = 16, 8, 2, 4
SLOTS = GROUPS * CELLS
ROWS = NV * CELLS
SEGMENTS = ((0, 384), (512, 352), (256, 384))
SEG = 384
Y_ORDER = (1, 2, 0, 3)


def tables():
    jk = np.arange(PLANE)
    bc = np.arange(FREQ)
    turns = (np.outer(jk // NV, bc // NC) + np.outer(jk % NV, bc % NC)) % NV
    keep = (bc % NC <= NV // 2).astype(np.float64)
    twice = np.where((bc % NC == 0) | (bc % NC == NV // 2), 1.0, 2.0) * keep
    cosine = np.round(np.cos(2 * np.pi * turns / NV), 12)
    sine = np.round(np.sin(2 * np.pi * turns / NV), 12)
    forward = np.concatenate([cosine * keep, -sine * keep], 1)
    inverse = np.concatenate([(cosine * twice).T, (-sine * twice).T], 0)
    row = np.arange(ROWS)
    i_at, i_cell = 3 * (row // CELLS % CHIPS) + row // (CELLS * CHIPS), row % CELLS
    a_at, a_cell = row % NV, row // NV
    turns = np.outer(a_at, i_at) % NV
    same = a_cell[:, None] == i_cell[None, :]
    cosine = np.round(np.cos(2 * np.pi * turns / NV), 12) * same
    sine = np.round(np.sin(2 * np.pi * turns / NV), 12) * same
    into_x = np.concatenate([cosine, sine], 0)
    from_x = np.concatenate([cosine.T, sine.T], 0)
    return tuple(jnp.asarray(t, dtype=BF16) for t in (forward, inverse, into_x, from_x))


def iota(shape, dim):
    return lax.broadcasted_iota(jnp.int32, shape, dim)


def dot(a, b):
    return jnp.dot(a, b, preferred_element_type=F32)


def kernel(
    dist, level_hbm, kernel_a, kernel_b, kernel_c, forward_hbm, inverse_hbm, into_hbm, from_hbm, read, packed, placer,
    ext, face, halo, edge_out, edge_in, values, send, recv, back, forward, inverse, into_x, from_x, raw, spread, sym, level,
    local_sem, table_sem, hop_sem, face_send, face_recv, send_sem, recv_sem, back_send, back_recv,
):
    me = lax.axis_index("vel")
    my_x, my_y = lax.axis_index("cx"), lax.axis_index("cy")
    nx, ny = lax.axis_size("cx"), lax.axis_size("cy")
    x_low, x_high = {"cx": lax.rem(my_x + nx - 1, nx)}, {"cx": lax.rem(my_x + 1, nx)}
    y_low, y_high = {"cy": lax.rem(my_y + ny - 1, ny)}, {"cy": lax.rem(my_y + 1, ny)}
    falling = me < GROUPS // 2
    even = lax.rem(me, 2) == 0

    barrier = pltpu.get_barrier_semaphore()
    twin = me + 1 - 2 * lax.rem(me, 2)
    near = [twin] + [lax.rem(m + d, GROUPS) for m in (me, twin) for d in (2, GROUPS - 2)]
    beside = [x_low, x_high, y_low, y_high] + [{"vel": v} for v in near]
    for there in beside:
        pl.semaphore_signal(barrier, inc=1, device_id=there, device_id_type=MESH)
    loads = [
        pltpu.make_async_copy(
            dist.at[8 * s : 8 * s + 8], ext.at[1:9, 1:5, 4 * s : 4 * s + 4], local_sem.at[s]
        )
        for s in range(2)
    ]
    loads += [
        pltpu.make_async_copy(dist.at[8], ext.at[9, 1:5, 0:4], local_sem.at[2]),
        pltpu.make_async_copy(dist.at[7], ext.at[0, 1:5, 4:8], local_sem.at[3]),
        pltpu.make_async_copy(level_hbm, level, local_sem.at[4]),
    ]
    for load in loads:
        load.start()
    table_loads = [
        pltpu.make_async_copy(src, dst, table_sem.at[k])
        for k, (src, dst) in enumerate(
            (
                (forward_hbm, forward), (inverse_hbm, inverse), (into_hbm, into_x), (from_hbm, from_x),
                (kernel_a, raw.at[0:PLANE]), (kernel_b, raw.at[PLANE : 2 * PLANE]),
                (kernel_c, raw.at[2 * PLANE : 3 * PLANE]),
            )
        )
    ]

    order = [(dz, t) for dz in (4, 3, -3, 2, -2, 1, -1, 0) for t in (0, 1) if (dz, t) != (0, 0)]

    def partner(d):
        return lax.rem((twin if d[1] else me) + 2 * d[0] + GROUPS, GROUPS)


    def remote(src, dst, send_at, recv_at, there):
        return pltpu.make_async_remote_copy(
            src_ref=src, dst_ref=dst, send_sem=send_at, recv_sem=recv_at,
            device_id=there, device_id_type=MESH,
        )

    def x_copy(up):
        return remote(edge_out, edge_in, face_send.at[0], face_recv.at[0], x_low if up else x_high)

    def y_copies(is_even):
        outer = remote(
            face.at[0:2], halo.at[0:2], face_send.at[1], face_recv.at[1],
            y_low if is_even else y_high,
        )
        middle = remote(
            face.at[2], halo.at[2], face_send.at[2], face_recv.at[2],
            y_high if is_even else y_low,
        )
        return outer, middle

    for load in loads[:2]:
        load.wait()
    outer_y = jnp.where(even, 1, 4)
    for k, (first, width) in enumerate(SEGMENTS):
        y = 5 - outer_y if k == 2 else outer_y
        face[k, :, 0:width] = ext[1:9, y, :, first : first + width].reshape(64, width).astype(BF16)

    for load in loads[2:]:
        load.wait()
    edge = jnp.where(falling, ext[1, 1:5, 0:4], ext[8, 1:5, 4:8])
    edge_out[...] = edge.reshape(16, LOCAL).astype(BF16)

    pl.semaphore_wait(barrier, len(beside))
    for case in (True, False):

        @pl.when(even == case)
        def _():
            for copy in y_copies(case):
                copy.start()

    for case in (True, False):

        @pl.when(falling == case)
        def _():
            x_copy(case).start()

    for load in table_loads:
        load.start()
    def tell(k):
        for side, d in enumerate((2, GROUPS - 2)):
            pl.semaphore_signal(
                hop_sem.at[2 * k + side], inc=1, device_id={"vel": lax.rem(me + d, GROUPS)},
                device_id_type=MESH,
            )

    def hear(k):
        for side in range(2):
            pl.semaphore_wait(hop_sem.at[2 * k + side], 1)

    tell(0)

    levels = jnp.concatenate([level[y] for y in range(4)], axis=0).astype(F32).astype(BF16)
    r = iota((16, 256), 1)
    row = iota((16, 256), 0)
    x_hot = (row == lax.rem(r // 4, 2) * 8 + r // 32).astype(F32).astype(BF16)
    y_rank = lax.rem(r // 8, 4)
    yz_hot = row == jnp.where(y_rank < 2, y_rank + 1, 3 * y_rank - 6) * 4 + lax.rem(r, 4)
    by_yz = dot(levels, x_hot)
    level_row = jnp.sum(jnp.where(yz_hot, by_yz, 0.0), axis=0, keepdims=True)
    active = (level_row > 0.5).astype(F32)
    upto = (iota((256, 256), 0) <= iota((256, 256), 1)).astype(F32).astype(BF16)
    slot = dot(jnp.broadcast_to(active, (8, 256)).astype(BF16), upto)[0:1] - 1.0
    hot = (
        (iota((128, 256), 0).astype(F32) == slot) & (jnp.broadcast_to(active, (128, 256)) > 0.5)
    ).astype(F32)
    picker = hot.astype(BF16)
    placer[...] = (hot * (0.25 * level_row)).astype(BF16)

    lane = iota((1, LOCAL), 1) + me * LOCAL

    def speed(index):
        return 0.3 * (2.0 * index.astype(F32) - (NV - 1)) / (NV - 1)

    c_x = speed(lane // PLANE)
    c_y = speed(lax.rem(lane // NV, NV))
    c_z = speed(lax.rem(lane, NV))
    shape = (8, LOCAL)
    a_x, a_y, a_z = (jnp.broadcast_to(jnp.abs(c), shape) for c in (c_x, c_y, c_z))
    up_y, up_z = (jnp.broadcast_to(c, shape) > 0.0 for c in (c_y, c_z))
    z_at = lax.rem(iota(shape, 0), 4)
    first_z, last_z = z_at == 0, z_at == 3
    step_x = jnp.where(falling, 1, -1)

    def keep(x, pair, done):
        at = pl.multiple_of(32 * x + 16 * pair, 16)
        values[pl.ds(at, 16), :] = jnp.concatenate(done, axis=0).astype(BF16)

    def along_xz(x, y):
        f = ext[x + 1, y + 1]
        low = jnp.where(first_z, pltpu.roll(f, 5, 0), pltpu.roll(f, 1, 0))
        high = jnp.where(last_z, pltpu.roll(f, 3, 0), pltpu.roll(f, 7, 0))
        flux = a_x * (f - ext[x + 1 + step_x, y + 1])
        return f - (flux + a_z * (f - jnp.where(up_z, low, high)))

    def along_y(x, y):
        return a_y * (ext[x + 1, y + 1] - jnp.where(up_y, ext[x + 1, y], ext[x + 1, y + 2]))

    def before_halo(x):
        done = []
        for rank, y in enumerate(Y_ORDER):
            left = along_xz(x, y)
            if rank < 2:
                left = left - along_y(x, y)
                done.append(left)
            read[x, rank] = left
        keep(x, 0, done)

    first_inner = jnp.where(falling, 0, 1)

    def inner(k, _):
        before_halo(first_inner + k)
        return 0

    hear(0)
    tell(1)
    lax.fori_loop(0, 7, inner, 0)
    hear(1)
    tell(2)

    for case in (True, False):

        @pl.when(even == case)
        def _():
            for copy in y_copies(case):
                copy.wait()

    outer_halo = jnp.where(even, 5, 0)
    for k, (first, width) in enumerate(SEGMENTS):
        y = 5 - outer_halo if k == 2 else outer_halo
        ext[1:9, y, :, first : first + width] = halo[k, :, 0:width].astype(F32).reshape(8, 8, width)

    for case in (True, False):

        @pl.when(falling == case)
        def _():
            x_copy(case).wait()

    edge = edge_in[...].astype(F32).reshape(4, 4, LOCAL)
    ext[9, 1:5, 4:8] = edge
    ext[0, 1:5, 0:4] = edge

    before_halo(jnp.where(falling, 7, 0))

    def outer(x, _):
        done = []
        for rank in (2, 3):
            evolved = read[x, rank] - along_y(x, Y_ORDER[rank])
            read[x, rank] = evolved
            done.append(evolved)
        keep(x, 1, done)
        return 0

    lax.fori_loop(0, 8, outer, 0)

    def by_place(ref, turn, device):
        return ref.at[turn, lax.rem(device, 2), device // 2]

    def onward(turn, d):
        there = partner(d)
        return remote(
            send.at[turn, there], by_place(recv, turn, me), send_sem.at[turn], recv_sem.at[turn],
            {"vel": there},
        )

    def homeward(turn, d):
        there = partner(d)
        return remote(
            by_place(back, turn, there), packed.at[turn, me], back_send.at[turn], back_recv.at[turn],
            {"vel": there},
        )

    def all_of(ref, turn, sem):
        pltpu.make_async_copy(ref.at[turn], ref.at[turn], sem.at[turn]).wait()

    def others_of(ref, turn, sem):
        pltpu.make_async_copy(
            ref.at[turn, 0 : GROUPS - 1], ref.at[turn, 0 : GROUPS - 1], sem.at[turn]
        ).wait()

    for turn in range(TURNS):
        chosen = dot(picker[SLOTS * turn : SLOTS * (turn + 1)], values[...])
        send[turn] = chosen.reshape(GROUPS, CELLS, LOCAL).astype(BF16)
        if turn == 0:
            hear(2)
        for d in order:
            onward(turn, d).start()
        pltpu.make_async_copy(send.at[turn, me], by_place(recv, turn, me), recv_sem.at[turn]).start()

    for load in table_loads:
        load.wait()

    for b in range(NV):
        spread[:, NV * b : NV * b + NV] = raw[pl.ds(b, 3 * NV, stride=NV), :]
    high = spread[...].astype(BF16)
    parts = jnp.concatenate([high, (spread[...] - high.astype(F32)).astype(BF16)], axis=0)
    at = iota((6 * NV, 6 * NV), 0)
    a_at = lax.rem(at, NV)
    turn = (iota((6 * NV, 6 * NV), 1) == at - a_at + lax.rem(NV - a_at, NV)).astype(F32).astype(BF16)
    turned = dot(turn, parts).astype(BF16)
    lane_b, lane_c = iota((1, FREQ), 1) // NC, lax.rem(iota((1, FREQ), 1), NC)
    used = lane_c <= NV // 2
    same = jnp.where(used, lane_b * NV + lane_c, -1)
    other = jnp.where(used, lax.rem(NV - lane_b, NV) * NV + lax.rem(NV - lane_c, NV), -1)
    pick = iota((PLANE, FREQ), 0)
    both = dot(parts, (pick == same).astype(F32).astype(BF16)) + dot(
        turned, (pick == other).astype(F32).astype(BF16)
    )
    sym[...] = (both[: 3 * NV] + both[3 * NV :]) * (0.5 / float(NV**3))

    for turn in range(TURNS):
        all_of(recv, turn, recv_sem)
        left, right = (
            recv[turn, core].astype(F32).reshape(CHIPS * CELLS, LOCAL) for core in range(2)
        )
        cells = jnp.concatenate(
            [
                left[:, :PLANE],
                jnp.concatenate([left[:, PLANE:], right[:, :HALF]], axis=1),
                right[:, HALF:],
            ],
            axis=0,
        )
        section = dot(cells.astype(BF16), forward[...]).astype(BF16)
        turned = dot(into_x[...], section)
        spec_re = turned[:ROWS, :FREQ] + turned[ROWS:, FREQ:]
        spec_im = turned[:ROWS, FREQ:] - turned[ROWS:, :FREQ]
        spectra = []
        for k in range(3):
            weights = sym[k * NV : (k + 1) * NV]
            weights = jnp.concatenate([weights] * CELLS, axis=0)
            weighted = jnp.concatenate([spec_re * weights, spec_im * weights], axis=1).astype(BF16)
            turned = dot(from_x[...], weighted)
            spectra.append(
                jnp.concatenate(
                    [
                        turned[:ROWS, :FREQ] - turned[ROWS:, FREQ:],
                        turned[:ROWS, FREQ:] + turned[ROWS:, :FREQ],
                    ],
                    axis=1,
                ).astype(BF16)
            )
        filtered = dot(jnp.concatenate(spectra, axis=0), inverse[...])
        terms = filtered[:ROWS] * filtered[ROWS : 2 * ROWS] - cells * filtered[2 * ROWS :]
        third = CHIPS * CELLS
        low, middle, high = (terms[third * q : third * q + third] for q in range(3))
        sides = (
            jnp.concatenate([low, middle[:, :HALF]], axis=1),
            jnp.concatenate([middle[:, HALF:], high], axis=1),
        )
        for core in range(2):
            back[turn, core] = sides[core].reshape(CHIPS, CELLS, LOCAL).astype(BF16)
        for d in order:
            homeward(turn, d).start()
        pltpu.make_async_copy(
            by_place(back, turn, me), packed.at[turn, me], back_recv.at[turn]
        ).start()

    def rates(first, last):
        terms = [
            packed[turn].astype(F32).reshape(SLOTS, LOCAL).astype(BF16) for turn in range(first, last)
        ]
        given = lax.dot_general(
            placer[SLOTS * first : SLOTS * last, :], jnp.concatenate(terms, axis=0),
            (((0,), (0,)), ((), ())), preferred_element_type=F32,
        )
        return given.reshape(8, 4, 8, LOCAL)

    for turn in range(TURNS - 1):
        all_of(packed, turn, back_recv)
    read[...] = read[...] + rates(0, TURNS - 1)
    all_of(packed, TURNS - 1, back_recv)
    for turn in range(TURNS):
        others_of(send, turn, send_sem)
        others_of(packed, turn, back_send)


def put_out(read, packed, placer, out, ready, sem):
    terms = packed[TURNS - 1].astype(F32).reshape(SLOTS, LOCAL).astype(BF16)
    given = lax.dot_general(
        placer[SLOTS * (TURNS - 1) : SLOTS * TURNS, :], terms, (((0,), (0,)), ((), ())),
        preferred_element_type=F32,
    ).reshape(8, 4, 8, LOCAL)
    copies = []
    for k in range(4):
        rows = slice(2 * k, 2 * k + 2)
        evolved = read[rows] + given[rows]
        for part in range(2):
            here = slice(8 * part + 2 * k, 8 * part + 2 * k + 2)
            for rank, y in enumerate(Y_ORDER):
                ready[here, y] = evolved[:, rank, 4 * part : 4 * part + 4]
            copies.append(pltpu.make_async_copy(ready.at[here], out.at[here], sem.at[2 * k + part]))
            copies[-1].start()
    for copy in copies:
        copy.wait()


def in_hbm(array):
    return pltpu.with_memory_space_constraint(array, pltpu.MemorySpace.HBM)


def per_device(distribution, refine_level, gain_one, gain_two, loss_kernel):
    constants = tables()
    kernels = [k.reshape(PLANE, NV) for k in (gain_one, gain_two, loss_kernel)]
    hbm = pl.BlockSpec(memory_space=pltpu.MemorySpace.HBM)
    vmem = pl.BlockSpec(memory_space=pltpu.VMEM)
    dma = pltpu.SemaphoreType.DMA
    whole = [
        ((8, 4, 8, LOCAL), F32), ((TURNS, GROUPS, CELLS, LOCAL), BF16), ((TURNS * SLOTS, 256), BF16),
    ]
    parts = pl.pallas_call(
        kernel,
        out_shape=[pltpu.VMEM(*one) for one in whole],
        in_specs=[hbm] * 9,
        out_specs=[vmem] * 3,
        scratch_shapes=[
            pltpu.VMEM((10, 6, 8, LOCAL), F32),
            pltpu.VMEM((3, 64, SEG), BF16),
            pltpu.VMEM((3, 64, SEG), BF16),
            pltpu.VMEM((16, LOCAL), BF16),
            pltpu.VMEM((16, LOCAL), BF16),
            pltpu.VMEM((256, LOCAL), BF16),
            pltpu.VMEM((TURNS, GROUPS, CELLS, LOCAL), BF16),
            pltpu.VMEM((TURNS, 2, CHIPS, CELLS, LOCAL), BF16),
            pltpu.VMEM((TURNS, 2, CHIPS, CELLS, LOCAL), BF16),
            pltpu.VMEM((PLANE, 2 * FREQ), BF16),
            pltpu.VMEM((2 * FREQ, PLANE), BF16),
            pltpu.VMEM((2 * ROWS, ROWS), BF16),
            pltpu.VMEM((2 * ROWS, ROWS), BF16),
            pltpu.VMEM((3 * PLANE, NV), F32),
            pltpu.VMEM((3 * NV, PLANE), F32),
            pltpu.VMEM((3 * NV, FREQ), F32),
            pltpu.VMEM((4, 4, 16), jnp.int32),
            dma((5,)), dma((7,)), pltpu.SemaphoreType.REGULAR((6,)), dma((3,)), dma((3,)),
            *[dma((TURNS,))] * 4,
        ],
        compiler_params=pltpu.CompilerParams(
            collective_id=0, has_side_effects=True, vmem_limit_bytes=48 << 20
        ),
    )(*map(in_hbm, (distribution, refine_level.transpose(1, 2, 0), *kernels, *constants)))

    return pl.pallas_call(
        put_out,
        out_shape=pltpu.HBM(distribution.shape, F32),
        in_specs=[vmem] * 3,
        out_specs=hbm,
        scratch_shapes=[pltpu.VMEM(distribution.shape, F32), dma((8,))],
        compiler_params=pltpu.CompilerParams(vmem_limit_bytes=16 << 20),
    )(*(pltpu.with_memory_space_constraint(one, pltpu.MemorySpace.VMEM) for one in parts))


def solution(mesh):
    in_specs = (P("cx", "cy", None, "vel"), P("cx", "cy", None), P(), P(), P())
    return jax.shard_map(
        per_device, mesh=mesh, in_specs=in_specs,
        out_specs=P("cx", "cy", None, "vel"), check_vma=False,
    )
```
